256 devices in a mesh: grp: 32 (over z, y), tp: 8 (over x, core).
Axes of the slice: x: 4, y: 4, z: 8, core: 2. Of those that a mesh axis runs over, the one named last changes fastest.
Arguments:
- hidden: bfloat16 [24576, 4608], P('grp', 'tp'), as said below
- norm_gain: float32 [4608], replicated, may hold values from 0.1 to 1.9
- q_weight: bfloat16 [4608, 2048], P(None, 'tp'), as said below
- k_weight: bfloat16 [4608, 1024], P(None, 'tp'), as said below
- v_weight: bfloat16 [4608, 1024], P(None, 'tp'), may hold values from -0.09375 to 0.09375
- kv_pages: bfloat16 [16384, 16, 8, 256], P('grp', None, 'tp'), as said below
- page_table: int32 [512, 256], P('grp'), may hold values from 0 to 575
- cache_len: int32 [512], P('grp'), may hold values from 1 to 4096, as said below
- tree_parent: int32 [512, 48], P('grp'), may hold values from -1 to 46, as said below
- accept_node: int32 [512], P('grp'), may hold values from 0 to 47
- pair_slot: int32 [32, 2], P('grp'), may hold values from 0 to 15, as said below
- far_len: int32 [32, 2], replicated, may hold values from 1 to 4096, as said below
- far_table: int32 [64, 256], P('grp'), may hold values from 0 to 575
- mig_src: int32 [2048], P('grp'), may hold values from 0 to 31, as said below
- mig_page: int32 [2048], P('grp'), may hold values from 0 to 511
Outputs:
- attn_out: bfloat16 [24576, 2048], P('grp', 'tp')
- accepted: bfloat16 [2560, 8, 256], P('grp', 'tp')
The draws below stay inside these ranges and needn't reach their ends.
Inputs may be any that keep to these rules, and one draw needn't show every extreme that they name: `hidden`: entries within 4 times a scale of order one, with column scales spread over a factor of ten. `q_weight`: entries within 4 / sqrt(4608). `k_weight`: entries within 9 / sqrt(4608). `kv_pages`: finite, of order one, some key entries larger. `cache_len`: some request has exactly 4096 cached tokens. `tree_parent`: node 0 is the root with parent -1; nodes are ordered by depth and each parent is an earlier node one level up; depths are at most 4 and every tree has a node of depth 4. `pair_slot`: the 2 slots of a group differ. `far_len`: some entry is exactly 4096. `mig_src`: never the receiving group itself; at most 4 of a group's entries name one source, and in every group exactly 4 name one source.
All inputs are finite; a program needn't handle non-finite values.
Results may differ from the reference program's by a relative error of at most 0.012.
Values may be sent and summed in bfloat16 or wider, within the bound.
A program may use at most 128 MiB of HBM per device.

```python
import jax
import jax.numpy as jnp
from jax import lax

D = 4608
QHEADS = 16
KVHEADS = 8
HEAD = 128
TREE = 48
PAGE = 16
MAXP = 256
LONG = 2
CAP = 4
ACCEPT = 5
REQ = 16
POOL = 512
MIGN = 64
SLOTS = 576
REQS = 512
TOKENS = 24576
N_GRP = 32


def draw_hidden(key, part):
    key = jax.random.fold_in(key, 11)
    column_key, row_key, value_key = jax.random.split(key, 3)
    column_scale = jnp.exp(jax.random.uniform(column_key, (D,), jnp.float32, -1.15, 1.15))
    row_scale = jnp.exp(jax.random.uniform(row_key, (TOKENS, 1), jnp.float32, -1.15, 1.15))
    values = jnp.clip(jax.random.normal(value_key, (TOKENS, D), jnp.float32), -4.0, 4.0)
    return (values * column_scale[None, :] * row_scale).astype(jnp.bfloat16)


def weight_pair(key):
    key = jax.random.fold_in(key, 23)
    query_key, noise_key = jax.random.split(key)
    query_part = jnp.clip(jax.random.normal(query_key, (D, QHEADS * HEAD), jnp.float32), -4.0, 4.0) * D ** (-0.5)
    paired = query_part.reshape(D, KVHEADS, 2, HEAD)
    noise = jnp.clip(jax.random.normal(noise_key, (D, KVHEADS, HEAD), jnp.float32), -4.0, 4.0) * D ** (-0.5)
    key_part = 0.6 * (paired[:, :, 0] + paired[:, :, 1]) + 0.5 * noise
    return (query_part, key_part.reshape(D, KVHEADS * HEAD))


def draw_q_weight(key, part):
    return weight_pair(key)[0].astype(jnp.bfloat16)


def draw_k_weight(key, part):
    return weight_pair(key)[1].astype(jnp.bfloat16)


def draw_kv_pages(key, part):
    key = jax.random.fold_in(key, 37)
    first_key, second_key = jax.random.split(key, 2)
    shape = (REQS // REQ * POOL, PAGE, KVHEADS, HEAD)
    key_half = 1.5 * jnp.clip(jax.random.normal(first_key, shape, jnp.float32), -5.0, 5.0)
    value_half = jnp.clip(jax.random.normal(second_key, shape, jnp.float32), -5.0, 5.0)
    return jnp.concatenate([key_half, value_half], -1).astype(jnp.bfloat16)


def draw_cache_len(key, part):
    key = jax.random.fold_in(key, 53)
    scale_key, length_key, where_key = jax.random.split(key, 3)
    groups = REQS // REQ
    ceiling_all = MAXP * PAGE
    factor = jax.random.randint(scale_key, (groups, 1), 1, 5)
    ceiling = jnp.maximum(ceiling_all * factor // 4, 1)
    lengths = jax.random.randint(length_key, (groups, REQ), 1, ceiling + 1).reshape(-1)
    target = jax.random.randint(where_key, (), 0, REQS)
    lengths = jnp.where(jnp.arange(REQS) == target, ceiling_all, lengths)
    return lengths.astype(jnp.int32)


def draw_far_len(key, part):
    key = jax.random.fold_in(key, 59)
    length_key, where_key = jax.random.split(key)
    groups = REQS // REQ
    ceiling_all = MAXP * PAGE
    lengths = jax.random.randint(length_key, (groups * LONG,), 1, ceiling_all + 1)
    target = jax.random.randint(where_key, (), 0, groups * LONG)
    lengths = jnp.where(jnp.arange(groups * LONG) == target, ceiling_all, lengths)
    return lengths.reshape(groups, LONG).astype(jnp.int32)


def draw_pair_slot(key, part):
    key = jax.random.fold_in(key, 61)
    groups = REQS // REQ

    def single(group_key):
        return jax.random.permutation(group_key, REQ)[:LONG]
    return jax.vmap(single)(jax.random.split(key, groups)).astype(jnp.int32)


def draw_tree_parent(key, part):
    key = jax.random.fold_in(key, 41)

    def single(tree_key):
        cut_key, pick_key = jax.random.split(tree_key)
        cuts = jnp.sort(jax.random.permutation(cut_key, TREE - 2)[:3] + 2).astype(jnp.int32)
        nodes = jnp.arange(TREE, dtype=jnp.int32)
        depths = (nodes >= 1).astype(jnp.int32) + (nodes >= cuts[0]).astype(jnp.int32) + (nodes >= cuts[1]).astype(jnp.int32) + (nodes >= cuts[2]).astype(jnp.int32)
        starts = jnp.concatenate([jnp.array([0, 1], jnp.int32), cuts, jnp.array([TREE], jnp.int32)])
        lower = starts[jnp.maximum(depths - 1, 0)]
        upper = jnp.maximum(starts[depths], lower + 1)
        picks = jax.random.randint(pick_key, (TREE,), lower, upper)
        return jnp.where(depths == 0, -1, picks).astype(jnp.int32)
    return jax.vmap(single)(jax.random.split(key, REQS))


def draw_mig_src(key, part):
    key = jax.random.fold_in(key, 71)
    groups = REQS // REQ

    def single(group, group_key):
        order_key, pick_key, shuffle_key = jax.random.split(group_key, 3)
        shuffled = jax.random.permutation(order_key, groups - 1).astype(jnp.int32)
        others = shuffled + (shuffled >= group).astype(jnp.int32)
        repeated = jnp.repeat(others[1:], CAP)
        picked = jax.random.permutation(pick_key, repeated)[:MIGN - CAP]
        entries = jnp.concatenate([jnp.full((CAP,), others[0], jnp.int32), picked])
        return jax.random.permutation(shuffle_key, entries)
    every = jax.vmap(single)(jnp.arange(groups, dtype=jnp.int32), jax.random.split(key, groups))
    return every.reshape(-1).astype(jnp.int32)


def set_ends(values, rng, smallest, top_value):
    longest = values.shape.index(max(values.shape))
    spots = []
    for shift in (0, 1):
        where = [jax.random.randint(jax.random.fold_in(rng, axis), (), 0, length) for axis, length in enumerate(values.shape)]
        where[longest] = (where[longest] + shift) % values.shape[longest]
        spots.append(tuple(where))
    return values.at[spots[0]].set(smallest).at[spots[1]].set(top_value)


def block_scale(own_key, dims, cuts, smallest, high):
    gain = 1.0
    for dim, parts in cuts:
        steps = jax.random.uniform(jax.random.fold_in(jax.random.fold_in(own_key, 6), dim), (parts,), jnp.float32, smallest / len(cuts), high / len(cuts))
        gain = gain * jnp.repeat(jnp.exp(steps), dims[dim] // parts).reshape((-1,) + (1,) * (len(dims) - 1 - dim))
    return gain


def centred(rng, shape, spread, most, cuts=(), held_as=jnp.bfloat16):
    values = spread * jax.random.normal(rng, shape, jnp.float32)
    if cuts:
        values = values * block_scale(rng, shape, cuts, -0.22, 0.18)
    return jnp.clip(values, -most, most).astype(held_as)


def setup_inputs(seed: int = 0) -> dict:
    seeds = jax.random.split(jax.random.key(seed), 16)
    hidden = draw_hidden(jax.random.fold_in(seeds[15], 71), 0)
    norm_gain = jnp.clip(1.0 + 0.18 * jax.random.normal(seeds[1], (D,), jnp.float32), 0.1, 1.9)
    q_weight = draw_q_weight(jax.random.fold_in(seeds[15], 71), 0)
    k_weight = draw_k_weight(jax.random.fold_in(seeds[15], 71), 0)
    v_weight = centred(seeds[4], (D, KVHEADS * HEAD), D ** -0.5, 0.09375, ((1, 8),))
    kv_pages = draw_kv_pages(jax.random.fold_in(seeds[15], 71), 0)
    page_table = set_ends(jax.random.randint(seeds[6], (REQS, MAXP), 0, SLOTS), jax.random.fold_in(seeds[6], 1), 0, SLOTS - 1).astype(jnp.int32)
    cache_len = draw_cache_len(jax.random.fold_in(seeds[15], 71), 0)
    tree_parent = draw_tree_parent(jax.random.fold_in(seeds[15], 71), 0)
    accept_node = set_ends(jax.random.randint(seeds[9], (REQS,), 0, TREE), jax.random.fold_in(seeds[9], 1), 0, TREE - 1).astype(jnp.int32)
    pair_slot = draw_pair_slot(jax.random.fold_in(seeds[15], 71), 0)
    far_len = draw_far_len(jax.random.fold_in(seeds[15], 71), 0)
    far_table = set_ends(jax.random.randint(seeds[12], (N_GRP * LONG, MAXP), 0, SLOTS), jax.random.fold_in(seeds[12], 1), 0, SLOTS - 1).astype(jnp.int32)
    mig_src = draw_mig_src(jax.random.fold_in(seeds[15], 71), 0)
    mig_page = set_ends(jax.random.randint(seeds[14], (N_GRP * MIGN,), 0, POOL), jax.random.fold_in(seeds[14], 1), 0, POOL - 1).astype(jnp.int32)
    return dict(hidden=hidden, norm_gain=norm_gain, q_weight=q_weight, k_weight=k_weight, v_weight=v_weight, kv_pages=kv_pages, page_table=page_table, cache_len=cache_len, tree_parent=tree_parent, accept_node=accept_node, pair_slot=pair_slot, far_len=far_len, far_table=far_table, mig_src=mig_src, mig_page=mig_page)


THETA_LOG = 9.210340371976184
SCORE_SCALE = 144.0 ** (-0.5)
LOGIT_CAP = 50.0
HIGHEST = lax.Precision.HIGHEST

def rotate(values, position):
    halfway = values.shape[-1] // 2
    angles = jnp.exp(-THETA_LOG * 2.0 * jnp.arange(halfway, dtype=jnp.float32) / values.shape[-1])
    phases = position.astype(jnp.float32)[:, None] * angles[None, :]
    cosine = jnp.cos(phases)[:, None, :]
    sine_part = jnp.sin(phases)[:, None, :]
    former = values[..., :halfway]
    latter = values[..., halfway:]
    return jnp.concatenate([former * cosine - latter * sine_part, latter * cosine + former * sine_part], -1)

def ancestry(parents):
    length = parents.shape[-1]
    labels = jnp.arange(length, dtype=jnp.int32)
    reached = (parents[..., :, None] == labels).astype(jnp.float32) + jnp.eye(length, dtype=jnp.float32)
    reached = jnp.minimum(jnp.einsum('nij,njk->nik', reached, reached, precision=HIGHEST), 1.0)
    reached = jnp.minimum(jnp.einsum('nij,njk->nik', reached, reached, precision=HIGHEST), 1.0)
    depths = lax.optimization_barrier(jnp.sum((reached > 0.5).astype(jnp.int32), -1)) - 1
    return (reached, depths)

def reference(hidden, norm_gain, q_weight, k_weight, v_weight, kv_pages, page_table, cache_len, tree_parent, accept_node, pair_slot, far_len, far_table, mig_src, mig_page):
    widened = hidden.astype(jnp.float32)
    row_scale = lax.rsqrt(lax.optimization_barrier(jnp.mean(widened * widened, axis=1)) + 1e-06)[:, None]
    scaled = (widened * norm_gain.astype(jnp.float32)[None, :]).astype(jnp.bfloat16)
    reached, depths = ancestry(tree_parent)
    slot_ids = jnp.arange(REQ, dtype=jnp.int32)
    matched = pair_slot[:, None, :] == slot_ids[None, :, None]
    far_own = lax.optimization_barrier(jnp.sum(jnp.where(matched, far_len[:, None, :], 0), -1)).reshape(-1)
    far_choice = lax.optimization_barrier(jnp.sum(jnp.where(matched, jnp.arange(LONG, dtype=jnp.int32)[None, None, :], 0), -1)).reshape(-1)
    long_flags = jnp.any(matched, -1).reshape(-1)
    position = ((cache_len + far_own)[:, None] + depths).reshape(-1)
    query_proj = jnp.dot(scaled, q_weight, preferred_element_type=jnp.float32) * row_scale
    queries = rotate(query_proj.reshape(TOKENS, QHEADS, HEAD), position).astype(jnp.bfloat16)
    key_proj = jnp.dot(scaled, k_weight, preferred_element_type=jnp.float32) * row_scale
    keys_new = rotate(key_proj.reshape(TOKENS, KVHEADS, HEAD), position).astype(jnp.bfloat16)
    value_proj = jnp.dot(scaled, v_weight, preferred_element_type=jnp.float32) * row_scale
    values_new = value_proj.astype(jnp.bfloat16).reshape(TOKENS, KVHEADS, HEAD)
    pools = kv_pages.reshape(N_GRP, POOL, PAGE, KVHEADS, 2 * HEAD)
    moved = pools[mig_src.reshape(N_GRP, MIGN), mig_page.reshape(N_GRP, MIGN)]
    extended = jnp.concatenate([pools, moved], 1)
    owners = jnp.arange(REQS, dtype=jnp.int32) // REQ
    offsets = jnp.arange(MAXP * PAGE, dtype=jnp.int32)

    def attend_one(packed):
        query_rows, key_rows, value_rows, table_row, own_length, tree_mask, owner, far_slot, long_flag = packed
        partner = owner + 1 - 2 * (owner % 2)
        own_cache = extended[owner, table_row].reshape(MAXP * PAGE, KVHEADS, 2 * HEAD)
        far_row = far_table[partner * LONG + far_slot]
        far_cache = extended[partner, far_row].reshape(MAXP * PAGE, KVHEADS, 2 * HEAD)
        far_length = far_len[owner, far_slot]
        all_keys = jnp.concatenate([own_cache[..., :HEAD], far_cache[..., :HEAD], key_rows], 0).astype(jnp.float32)
        all_values = jnp.concatenate([own_cache[..., HEAD:], far_cache[..., HEAD:], value_rows], 0).astype(jnp.float32)
        cache_ok = jnp.broadcast_to((offsets < own_length)[None, :], (TREE, MAXP * PAGE))
        far_ok = jnp.broadcast_to(((offsets < far_length) & long_flag)[None, :], (TREE, MAXP * PAGE))
        allowed = jnp.concatenate([cache_ok, far_ok, tree_mask > 0.5], 1)
        grouped = query_rows.reshape(TREE, KVHEADS, 2, HEAD).astype(jnp.float32)
        scores = jnp.einsum('igrd,tgd->igrt', grouped, all_keys, precision=HIGHEST) * SCORE_SCALE
        scores = LOGIT_CAP * jnp.tanh(scores / LOGIT_CAP)
        weights = jnp.where(allowed[:, None, None, :], jnp.exp(scores - LOGIT_CAP), 0.0)
        totals = lax.optimization_barrier(jnp.sum(weights, -1))
        rounded = weights.astype(jnp.bfloat16).astype(jnp.float32)
        mixed = jnp.einsum('igrt,tgd->igrd', rounded, all_values, precision=HIGHEST) / totals[..., None]
        return mixed.reshape(TREE, QHEADS * HEAD).astype(jnp.bfloat16)
    attn_out = lax.map(attend_one, (queries.reshape(REQS, TREE, QHEADS, HEAD), keys_new.reshape(REQS, TREE, KVHEADS, HEAD), values_new.reshape(REQS, TREE, KVHEADS, HEAD), page_table, cache_len, reached, owners, far_choice, long_flags)).reshape(TOKENS, QHEADS * HEAD)
    leaves = (jnp.arange(TREE, dtype=jnp.int32)[None, :] == accept_node[:, None]).astype(jnp.float32)
    lineage = jnp.einsum('rt,rtj->rj', leaves, reached, precision=HIGHEST)
    levels = (depths[:, None, :] == jnp.arange(ACCEPT, dtype=jnp.int32)[None, :, None]).astype(jnp.float32)
    picker = lineage[:, None, :] * levels
    fresh_rows = jnp.concatenate([keys_new, values_new], -1).reshape(REQS, TREE, KVHEADS * 2 * HEAD).astype(jnp.float32)
    accepted = jnp.einsum('rpt,rtc->rpc', picker, fresh_rows, precision=HIGHEST).astype(jnp.bfloat16).reshape(REQS * ACCEPT, KVHEADS, 2 * HEAD)
    return (attn_out, accepted)
```

```python
import jax
import jax.numpy as jnp
from jax import lax
from jax.experimental import pallas as pl
from jax.experimental.pallas import tpu as pltpu
from jax.sharding import PartitionSpec as P

CAP = 4
ACCEPT = 5
THETA_LOG = 9.210340371976184
PRE = 144.0 ** (-0.5) / 50.0
LOGIT_CAP = 50.0
POST = 50.0 * 1.4426950408889634
BLOCK_PAGES = 32
F32 = jnp.float32
BF16 = jnp.bfloat16


def nt(a, b):
    return lax.dot_general(a, b, (((1,), (1,)), ((), ())), preferred_element_type=F32)


def nn(a, b):
    return lax.dot_general(a, b, (((1,), (0,)), ((), ())), preferred_element_type=F32)


def weigh(scores):
    return jnp.exp2(jnp.tanh(scores * PRE) * POST)


def fold(weights):
    total = weights[:, 0:128]
    for part in range(1, weights.shape[1] // 128):
        total = total + weights[:, part * 128 : part * 128 + 128]
    return total


def load_pages(pages, table, row, first, count):
    loaded = [pages[table[row, first + number]] for number in range(count)]
    return jnp.concatenate(loaded, 0)


def page_block(query, pages, table, row, first, valid, acc, summed):
    size = pages.shape[1]
    both = load_pages(pages, table, row, first, BLOCK_PAGES)
    weights = weigh(nt(query, both[:, 0:128]))
    if valid is not None:
        where = lax.broadcasted_iota(jnp.int32, (1, BLOCK_PAGES * size), 1)
        weights = jnp.where(where < valid, weights, 0.0)
    summed = summed + fold(weights)
    acc = acc + nn(weights.astype(BF16), both[:, 128:256])
    return acc, summed


def page_loop(query, pages, table, row, length):
    span = BLOCK_PAGES * pages.shape[1]
    zero = jnp.zeros((query.shape[0], 128), F32)

    def step(number, state):
        return page_block(query, pages, table, row, number * BLOCK_PAGES, None, *state)

    full = lax.div(length, span)
    return full, lax.fori_loop(0, full, step, (zero, zero))


def page_rest(query, pages, table, row, full, length, state):
    span = BLOCK_PAGES * pages.shape[1]
    width = table.shape[1]
    first = jnp.minimum(full * BLOCK_PAGES, width - BLOCK_PAGES)
    return page_block(query, pages, table, row, first, length - full * span, *state)


def fill_pages(slots, kv_hbm, moved_hbm, pages, moved, sems):
    pool = kv_hbm.shape[0]
    first = pltpu.make_async_copy(kv_hbm, pages.at[pl.ds(0, pool)], sems.at[0])
    second = pltpu.make_async_copy(moved_hbm, moved, sems.at[1])
    first.start()
    second.start()
    first.wait()
    second.wait()
    for number in range(slots.shape[0]):
        pages[pool + number] = moved[slots[number]]


def far_kernel(slots, table, lens, kv_hbm, moved_hbm, q_ref, acc_ref, sum_ref, pages, moved, sems):
    fill_pages(slots, kv_hbm, moved_hbm, pages, moved, sems)
    for j in range(q_ref.shape[0]):
        query = q_ref[j]
        full, state = page_loop(query, pages, table, j, lens[j])
        acc, summed = page_rest(query, pages, table, j, full, lens[j], state)
        acc_ref[j] = acc
        sum_ref[j] = summed


def own_kernel(
    slots, table, lens, pair, leaf, kv_hbm, moved_hbm, q_ref, new_ref, mask_ref, facc_ref, fsum_ref,
    out_ref, path_ref, pages, moved, sems,
):
    fill_pages(slots, kv_hbm, moved_hbm, pages, moved, sems)
    tree = mask_ref.shape[1]

    def request(r, carry):
        rows = pl.ds(pl.multiple_of(r * tree, tree), tree)
        query = jnp.concatenate([q_ref[rows, 0:128], q_ref[rows, 128:256]], 0)
        length = lens[r]
        full, state = page_loop(query, pages, table, r, length)
        acc, summed = page_rest(query, pages, table, r, full, length, state)
        new = new_ref[rows, :]
        mask = mask_ref[r]
        weights = weigh(nt(query, new[:, 0:128])) * jnp.concatenate([mask, mask], 0)
        acc = acc + nn(weights.astype(BF16), new[:, 128:256])
        for j in range(2):
            mine = jnp.where(pair[0, j] == r, 1.0, 0.0)
            acc = acc + mine * facc_ref[j]
            summed = summed + mine * fsum_ref[j]
        total = jnp.sum(summed, -1, keepdims=True) + jnp.sum(weights, -1, keepdims=True)
        mixed = (acc / total).astype(BF16)
        out_ref[rows, 0:128] = mixed[0:tree]
        out_ref[rows, 128:256] = mixed[tree:]
        ones = jnp.ones((8, tree), F32)
        depth = nt(ones.astype(BF16), mask.astype(BF16)) - 1.0
        levels = lax.broadcasted_iota(jnp.int32, (8, tree), 0).astype(F32)
        lineage = mask_ref[r, pl.ds(leaf[r], 1), :]
        picker = jnp.where(depth == levels, 1.0, 0.0) * lineage
        path_ref[r] = nn(picker.astype(BF16), new).astype(BF16)
        return carry

    lax.fori_loop(0, lens.shape[0], request, 0)


def smem():
    return pl.BlockSpec(memory_space=pltpu.SMEM)


def anyspace():
    return pl.BlockSpec(memory_space=pl.ANY)


def vmem():
    return pl.BlockSpec(memory_space=pltpu.VMEM)


def page_scratch(kv, moved, slots):
    return [
        pltpu.VMEM((kv.shape[0] + slots.shape[0],) + kv.shape[1:], BF16),
        pltpu.VMEM(moved.shape, BF16),
        pltpu.SemaphoreType.DMA((2,)),
    ]


def attend_far(slots, table, lens, kv, moved, queries):
    shape = jax.ShapeDtypeStruct(queries.shape, F32)
    return pl.pallas_call(
        far_kernel,
        out_shape=(shape, shape),
        in_specs=[smem(), smem(), smem(), anyspace(), anyspace(), vmem()],
        out_specs=(vmem(), vmem()),
        scratch_shapes=page_scratch(kv, moved, slots),
        compiler_params=pltpu.CompilerParams(vmem_limit_bytes=40 << 20),
        name="attend_far",
    )(slots, table, lens, kv, moved, queries)


def attend_own(slots, table, lens, pair, leaf, kv, moved, queries, fresh, mask, facc, fsum):
    requests = lens.shape[0]
    return pl.pallas_call(
        own_kernel,
        out_shape=(
            jax.ShapeDtypeStruct(queries.shape, BF16),
            jax.ShapeDtypeStruct((requests, 8, 256), BF16),
        ),
        in_specs=[smem()] * 5 + [anyspace(), anyspace()] + [vmem()] * 5,
        out_specs=(vmem(), vmem()),
        scratch_shapes=page_scratch(kv, moved, slots),
        compiler_params=pltpu.CompilerParams(vmem_limit_bytes=40 << 20),
        name="attend_own",
    )(slots, table, lens, pair, leaf, kv, moved, queries, fresh, mask, facc, fsum)


def partner(value, axis):
    pairs = [(source, source ^ 1) for source in range(lax.axis_size(axis))]
    return lax.ppermute(value, axis, pairs)


def rotate(values, position):
    halfway = values.shape[-1] // 2
    angles = jnp.exp(-THETA_LOG * 2.0 * jnp.arange(halfway, dtype=F32) / values.shape[-1])
    phases = position.astype(F32)[:, None] * angles[None, :]
    cosine = jnp.cos(phases)[:, None, :]
    sine = jnp.sin(phases)[:, None, :]
    former = values[..., :halfway]
    latter = values[..., halfway:]
    return jnp.concatenate([former * cosine - latter * sine, latter * cosine + former * sine], -1)


def ancestry(parents):
    length = parents.shape[-1]
    labels = jnp.arange(length, dtype=jnp.int32)
    reached = (parents[..., :, None] == labels).astype(BF16) + jnp.eye(length, dtype=BF16)
    for _ in range(2):
        reached = jnp.minimum(
            jnp.einsum("nij,njk->nik", reached, reached, preferred_element_type=F32), 1.0
        ).astype(BF16)
    reached = reached.astype(F32)
    depths = jnp.sum(reached, -1).astype(jnp.int32) - 1
    return reached, depths


def body(
    hidden, norm_gain, q_weight, k_weight, v_weight, kv_pages, page_table, cache_len, tree_parent,
    accept_node, pair_slot, far_len, far_table, mig_src, mig_page,
):
    token_rows = hidden.shape[0]
    requests, tree = tree_parent.shape
    pool, page_size, _, entry = kv_pages.shape
    migrations = mig_src.shape[0]
    groups = lax.axis_size("grp")
    myself = lax.axis_index("grp")
    kv = kv_pages.reshape(pool, page_size, entry)
    order = jnp.arange(migrations, dtype=jnp.int32)
    rank = jnp.sum(
        ((mig_src[:, None] == mig_src[None, :]) & (order[:, None] > order[None, :])).astype(jnp.int32), -1
    )
    slots = mig_src * CAP + rank
    wanted = jnp.max(
        jnp.where(
            slots[None, :] == jnp.arange(groups * CAP, dtype=jnp.int32)[:, None], mig_page[None, :], 0
        ),
        -1,
    ).reshape(groups, CAP)
    asked = lax.all_to_all(wanted, "grp", split_axis=0, concat_axis=0, tiled=True)
    outgoing = kv[asked.reshape(-1)].reshape(groups, CAP, page_size, entry)
    moved = lax.all_to_all(outgoing, "grp", split_axis=0, concat_axis=0, tiled=True)
    moved = moved.reshape(groups * CAP, page_size, entry)
    widened = lax.all_gather(hidden, "tp", axis=1, tiled=True).astype(F32)
    scaled = (widened * norm_gain[None, :]).astype(BF16)
    row_scale = lax.rsqrt(jnp.mean(widened * widened, 1) + 1e-06)[:, None]
    reached, depths = ancestry(tree_parent)
    far_mine = lax.dynamic_index_in_dim(far_len, myself, 0, keepdims=False)
    far_theirs = lax.dynamic_index_in_dim(far_len, myself ^ 1, 0, keepdims=False)
    matched = jnp.arange(requests, dtype=jnp.int32)[:, None] == pair_slot
    far_own = jnp.sum(jnp.where(matched, far_mine[None, :], 0), 1)
    position = ((cache_len + far_own)[:, None] + depths).reshape(-1)
    dot = lambda weight: jnp.dot(scaled, weight, preferred_element_type=F32) * row_scale
    queries = rotate(dot(q_weight).reshape(token_rows, 2, 128), position)
    queries = queries.astype(BF16).reshape(token_rows, 256)
    keys_new = rotate(dot(k_weight).reshape(token_rows, 1, 128), position)
    keys_new = keys_new.astype(BF16).reshape(token_rows, 128)
    fresh = jnp.concatenate([keys_new, dot(v_weight).astype(BF16)], 1)
    long_queries = queries.reshape(requests, tree, 2, 128).transpose(0, 2, 1, 3)
    long_queries = long_queries.reshape(requests, 2 * tree, 128)[pair_slot[0]]
    visitors = partner(long_queries, "grp")
    facc, fsum = attend_far(slots, far_table, far_theirs, kv, moved, visitors)
    facc = partner(facc, "grp")
    fsum = partner(fsum, "grp")
    out, path = attend_own(
        slots, page_table, cache_len, pair_slot, accept_node, kv, moved, queries, fresh, reached, facc, fsum
    )
    return out, path[:, :ACCEPT].reshape(requests * ACCEPT, 1, entry)


def solution(mesh):
    in_specs = (
        P("grp", "tp"),
        P(),
        P(None, "tp"),
        P(None, "tp"),
        P(None, "tp"),
        P("grp", None, "tp", None),
        P("grp", None),
        P("grp"),
        P("grp", None),
        P("grp"),
        P("grp", None),
        P(),
        P("grp", None),
        P("grp"),
        P("grp"),
    )
    out_specs = (P("grp", "tp"), P("grp", "tp", None))
    return jax.shard_map(body, mesh=mesh, in_specs=in_specs, out_specs=out_specs, check_vma=False)
```

```python
import functools

import jax
import jax.numpy as jnp
from jax import lax
from jax.experimental import pallas as pl
from jax.experimental.pallas import tpu as pltpu
from jax.sharding import PartitionSpec as P

CAP = 4
ACCEPT = 5
THETA_LOG = 9.210340371976184
PRE = 144.0 ** (-0.5) / 50.0
POST = 50.0 * 1.4426950408889634
PARTS = 4
ITEM_PAGES = 64
EARLY = 4
F32 = jnp.float32
BF16 = jnp.bfloat16
I32 = jnp.int32
MESH = pl.DeviceIdType.MESH


def nt(a, b):
    return lax.dot_general(a, b, (((1,), (1,)), ((), ())), preferred_element_type=F32)


def nn(a, b):
    return lax.dot_general(a, b, (((1,), (0,)), ((), ())), preferred_element_type=F32)


def tn(a, b):
    return lax.dot_general(a, b, (((0,), (0,)), ((), ())), preferred_element_type=F32)


def weigh(scores):
    return jnp.exp2(jnp.tanh(scores * PRE) * POST)


def kernel(
    groups, share,
    table_hbm, lens_hbm, pair_hbm, leaf_hbm, far_len_hbm, far_table_hbm, src_hbm, page_hbm, gain_hbm, parents_hbm,
    hidden, kv_hbm, q_hbm, k_hbm, v_hbm,
    out, path,
    table, lens, pair, leaf, far_len, far_table, own_src, own_page, gain_rows, parents,
    tables, landed, wish, wish_smem, gain, xbuf, weights, acc, squares, xs, cosine, sine, pages, packed, arrived,
    masks, pickers, queries, fresh, scores, values, mixed, sums, far_query, far_ask, far_reply, far_back, row_reply,
    row_back,
    small_sem, local_sem, send_sem, recv_sem, table_send, table_recv, page_send, page_recv, far_send, far_recv,
):
    group = lax.axis_index("grp")
    me = lax.axis_index("tp")
    chips = share // 2
    chip, core = me // 2, me % 2
    right = ((chip + 1) % chips) * 2 + core
    left = ((chip + chips - 1) % chips) * 2 + core
    across = ((chip + 2) % chips) * 2 + core
    sibling = chip * 2 + 1 - core
    others = groups - 1
    mate = group + 1 - 2 * (group % 2)
    width, tokens = hidden.shape
    piece = width // PARTS
    pool, size = kv_hbm.shape[0:2]
    requests, tree = parents.shape
    migrations = own_src.shape[1]

    small = [
        pltpu.make_async_copy(source, target, small_sem.at[number])
        for number, (source, target) in enumerate(
            (
                (src_hbm, own_src),
                (page_hbm, own_page),
                (gain_hbm, gain_rows),
                (parents_hbm, parents),
                (table_hbm, table),
                (lens_hbm, lens),
                (pair_hbm, pair),
                (leaf_hbm, leaf),
                (far_len_hbm, far_len),
                (far_table_hbm, far_table),
            )
        )
    ]
    loads = [
        pltpu.make_async_copy(hidden, xbuf.at[me], local_sem.at[0]),
        pltpu.make_async_copy(kv_hbm, pages.at[pl.ds(0, pool)], local_sem.at[1]),
        pltpu.make_async_copy(q_hbm, weights.at[:, pl.ds(0, 256)], local_sem.at[2]),
        pltpu.make_async_copy(k_hbm, weights.at[:, pl.ds(256, 128)], local_sem.at[3]),
        pltpu.make_async_copy(v_hbm, weights.at[:, pl.ds(384, 128)], local_sem.at[4]),
    ]
    small[0].start()
    small[1].start()

    barrier = pltpu.get_barrier_semaphore()
    for peer in (left, right, sibling):
        pl.semaphore_signal(barrier, inc=1, device_id=(group, peer), device_id_type=MESH)

    def greet(number, carry):
        peer = (group + 1 + number) % groups
        pl.semaphore_signal(barrier, inc=1, device_id=(peer, me), device_id_type=MESH)
        return carry

    lax.fori_loop(0, others, greet, 0)
    small[0].wait()
    small[1].wait()
    tables[:, 0:migrations] = own_src[...]
    tables[:, migrations : 2 * migrations] = own_page[...]
    pl.semaphore_wait(barrier, 3 + others)

    sent = []

    def send(source, owner, part, peer):
        copy = pltpu.make_async_remote_copy(
            src_ref=source,
            dst_ref=xbuf.at[owner, pl.ds(part * piece, piece)],
            send_sem=send_sem.at[len(sent)],
            recv_sem=recv_sem.at[owner, part],
            device_id=(group, peer),
            device_id_type=MESH,
        )
        copy.start()
        sent.append(copy)

    def own_part(part):
        return hidden.at[pl.ds(part * piece, piece)]

    def held(owner, part):
        return xbuf.at[owner, pl.ds(part * piece, piece)]

    def arrive(owner, part):
        pltpu.make_async_remote_copy(
            src_ref=held(owner, part),
            dst_ref=held(owner, part),
            send_sem=send_sem.at[0],
            recv_sem=recv_sem.at[owner, part],
            device_id=(group, sibling),
            device_id_type=MESH,
        ).wait_recv()

    def table_copy(number):
        return pltpu.make_async_remote_copy(
            src_ref=tables,
            dst_ref=landed.at[number],
            send_sem=table_send,
            recv_sem=table_recv,
            device_id=((group + 1 + number) % groups, me),
            device_id_type=MESH,
        )

    def tell(number, carry):
        table_copy(number).start()
        return carry

    for part in range(PARTS):
        send(own_part(part), me, part, right)
        send(own_part(PARTS - 1 - part), me, PARTS - 1 - part, left)
        if part == 0:
            lax.fori_loop(0, others, tell, 0)
    for part in range(PARTS):
        send(own_part(part), me, part, sibling)
    for copy in loads + small[2:]:
        copy.start()

    def blank():
        pages[pl.ds(pool, migrations)] = jnp.zeros((migrations,) + pages.shape[1:], BF16)
        acc[...] = jnp.zeros_like(acc)
        squares[...] = jnp.zeros_like(squares)
        fresh[...] = jnp.zeros_like(fresh)
        row_reply[...] = jnp.zeros_like(row_reply)

    blank()
    table_all = pltpu.make_async_remote_copy(
        src_ref=landed,
        dst_ref=landed,
        send_sem=table_send,
        recv_sem=table_recv,
        device_id=(mate, me),
        device_id_type=MESH,
    )
    table_all.wait_recv()
    every = jnp.concatenate([landed[number] for number in range(others)] + [tables[...]], 0)
    wide_lane = lax.broadcasted_iota(I32, (groups, 128), 1)

    def before(marks):
        total = marks
        for shift in (1, 2, 4, 8, 16, 32):
            total = total + jnp.where(wide_lane >= shift, pltpu.roll(total, shift, 1), 0)
        return total - marks

    def across_lanes(value):
        for shift in (64, 32, 16, 8, 4, 2, 1):
            value = value + pltpu.roll(value, shift, 1)
        return value

    hits = jnp.where((every == group) & (wide_lane < migrations), 1, 0)
    ranks = before(hits)
    asked = pltpu.roll(every, migrations, 1)
    wanted = jnp.zeros((groups, 128), I32)
    for slot in range(CAP):
        chosen = across_lanes(jnp.where((hits == 1) & (ranks == slot), asked, 0))
        wanted = jnp.where(wide_lane == slot, chosen, wanted)
    mine = jnp.broadcast_to(tables[...], (groups, 128))
    source = lax.broadcasted_iota(I32, (groups, 128), 0)
    marks = jnp.where((source == mine) & (wide_lane < migrations), 1, 0)
    spot = marks * before(marks)
    for shift in (16, 8, 4, 2, 1):
        spot = spot + pltpu.roll(spot, shift, 0)
    spot = ((mine - group + groups) % groups - 1) * CAP + spot
    spot = jnp.minimum(jnp.maximum(spot, 0), others * CAP - 1)
    wish[0:groups, :] = wanted
    wish[groups : groups + 8, :] = jnp.where(wide_lane < migrations, spot, 0)[0:8]
    move = pltpu.make_async_copy(wish, wish_smem, local_sem.at[5])
    move.start()
    move.wait()
    loads[1].wait()

    def page_copy(number):
        return pltpu.make_async_remote_copy(
            src_ref=packed.at[pl.ds(number * CAP, CAP)],
            dst_ref=arrived.at[pl.ds(number * CAP, CAP)],
            send_sem=page_send,
            recv_sem=page_recv,
            device_id=((group + groups - 1 - number) % groups, me),
            device_id_type=MESH,
        )

    def pack(number, carry):
        for slot in range(CAP):
            packed[number * CAP + slot] = pages[wish_smem[number, slot]]
        page_copy(number).start()
        return carry

    lax.fori_loop(0, others, pack, 0)

    for copy in small[2:]:
        copy.wait()
    blocks = gain_rows.shape[0]
    columns = jnp.transpose(jnp.concatenate([gain_rows[...], jnp.zeros((128 - blocks, 128), F32)], 0))
    for block in range(blocks):
        gain[block * 128 : block * 128 + 128, :] = jnp.broadcast_to(columns[:, block : block + 1], (128, 128))

    def consume(owner, part):
        first = owner * width + part * piece
        total = squares[...]
        for strip in range(piece // 16):
            raw = xbuf[owner, pl.ds(part * piece + strip * 16, 16), :].astype(F32)
            factor = gain[pl.ds(first + strip * 16, 16), :]
            scaled = raw * jnp.concatenate([factor] * (tokens // 128), 1)
            xs[strip * 16 : strip * 16 + 16, :] = scaled.astype(BF16)
            square = raw * raw
            total = total + (square[0:8] + square[8:16])
        squares[...] = total
        block = weights[pl.ds(pl.multiple_of(first, 16), piece), :]
        for m in range(tokens // 256):
            at = slice(m * 256, m * 256 + 256)
            acc[at, :] = acc[at, :] + tn(xs[:, at], block)

    def turn_of(i, low, low_parts, high, high_parts):
        half = len(low_parts)
        step = i % (2 * half)
        is_low = step % 2 == 0
        owner = jnp.where(is_low, low, high)
        at_low = low_parts[0] + (step // 2) * (low_parts[1] - low_parts[0])
        at_high = high_parts[0] + (step // 2) * (high_parts[1] - high_parts[0])
        part = jnp.where(is_low, at_low, at_high)
        return jnp.where(i < 2 * half, owner, owner + 1 - 2 * (owner % 2)), part

    for load in (loads[0], loads[2], loads[3], loads[4]):
        load.wait()

    def take_own(i, carry):
        consume(me, i)
        return carry

    def take_sibling(i, carry):
        arrive(sibling, i)
        consume(sibling, i)
        return carry

    lax.fori_loop(0, PARTS, take_own, 0)
    lax.fori_loop(0, PARTS, take_sibling, 0)

    def take(low, low_parts, high, high_parts):
        half = len(low_parts)

        def direct(i, carry):
            consume(*turn_of(i, low, low_parts, high, high_parts))
            return carry

        def indirect(i, carry):
            owner, part = turn_of(i, low, low_parts, high, high_parts)
            arrive(owner, part)
            consume(owner, part)
            return carry

        lax.fori_loop(0, 2 * half, direct, 0)
        lax.fori_loop(2 * half, 4 * half, indirect, 0)

    ahead, behind = tuple(range(PARTS // 2)), tuple(range(PARTS // 2, PARTS))
    for number in range(PARTS // 2):
        arrive(left, ahead[number])
        send(held(left, ahead[number]), left, ahead[number], right)
        arrive(right, behind[-1 - number])
        send(held(right, behind[-1 - number]), right, behind[-1 - number], left)
    for number in range(PARTS // 2):
        send(held(left, ahead[number]), left, ahead[number], sibling)
        send(held(right, behind[-1 - number]), right, behind[-1 - number], sibling)

    node_row = lax.broadcasted_iota(I32, (tree, tree), 0)
    node_col = lax.broadcasted_iota(I32, (tree, tree), 1)
    eye = jnp.where(node_row == node_col, 1.0, 0.0).astype(BF16)
    levels = lax.broadcasted_iota(I32, (8, tree), 0).astype(F32)
    lane = lax.broadcasted_iota(I32, (1, 128), 1)
    angle = jnp.exp((lane % 64).astype(F32) * (-THETA_LOG * 2.0 / 128.0))
    turn = jnp.where(lane < 64, -1.0, 1.0)
    side = jnp.zeros((tree, 128 - tree), F32)

    def grow(number, carry):
        for half in range(2):
            r = number * 2 + half
            up = jnp.where(node_row == parents[pl.ds(r, 1), :], 1.0, 0.0).astype(BF16) + eye
            for _ in range(2):
                up = jnp.minimum(nn(up, up), 1.0).astype(BF16)
            reached = nt(eye, up)
            masks[r] = jnp.concatenate([reached, side], 1)
            depth_row = jnp.sum(up.astype(F32), 0, keepdims=True) - 1.0
            chosen = jnp.where(node_row == jnp.full((tree, tree), leaf[r], I32), reached, 0.0)
            lineage = jnp.sum(chosen, 0, keepdims=True)
            pickers[r] = jnp.where(depth_row == levels, lineage, 0.0)
            depth = jnp.sum(reached, -1, keepdims=True) - 1.0
            base = jnp.full((1, 128), lens[r], I32)
            for j in range(2):
                base = base + jnp.where(jnp.full((1, 128), pair[0, j], I32) == r, far_len[j, group], 0)
            phase = (base.astype(F32) + depth) * angle
            rows = pl.ds(pl.multiple_of(r * tree, tree), tree)
            cosine[rows, :] = jnp.cos(phase)
            sine[rows, :] = jnp.sin(phase) * turn
        return carry

    take(left, ahead, right, behind[::-1])
    lax.fori_loop(0, requests // 2, grow, 0)
    for number in range(PARTS // 2):
        arrive(left, behind[number])
        send(held(left, behind[number]), left, behind[number], sibling)
        arrive(right, ahead[-1 - number])
        send(held(right, ahead[-1 - number]), right, ahead[-1 - number], sibling)
    take(left, behind, right, ahead[::-1])

    page_all = pltpu.make_async_remote_copy(
        src_ref=packed,
        dst_ref=arrived,
        send_sem=page_send,
        recv_sem=page_recv,
        device_id=(mate, me),
        device_id_type=MESH,
    )
    page_all.wait_recv()
    for number in range(migrations):
        pages[pool + number] = arrived[wish_smem[groups, number]]

    for number in range(PARTS // 2):
        arrive(across, ahead[number])
        send(held(across, ahead[number]), across, ahead[number], sibling)
        arrive(across, behind[-1 - number])
        send(held(across, behind[-1 - number]), across, behind[-1 - number], sibling)
    take(across, ahead, across, behind[::-1])

    mean = lax.dot_general(
        squares[...], jnp.full((8, 128), 1.0 / (share * width), F32), (((0,), (0,)), ((), ())),
        precision=lax.Precision.HIGHEST, preferred_element_type=F32,
    )
    scale = lax.rsqrt(mean + 1e-06)
    cosine[...] = cosine[...] * scale
    sine[...] = sine[...] * scale
    fresh[0:tokens, 128:256] = (acc[:, 384:512] * scale).astype(BF16)

    def turned(rows, at):
        value = acc[rows, at : at + 128]
        return (value * cosine[rows, :] + pltpu.roll(value, 64, 1) * sine[rows, :]).astype(BF16)

    def finish(number, carry):
        for half in range(2):
            r = number * 2 + half
            rows = pl.ds(pl.multiple_of(r * tree, tree), tree)
            fresh[rows, 0:128] = turned(rows, 256)
            queries[r, 0:tree, :] = turned(rows, 0)
            queries[r, tree : 2 * tree, :] = turned(rows, 128)
        return carry

    lax.fori_loop(0, requests // 2, finish, 0)
    for j in range(2):
        far_query[j] = queries[pair[0, j]]

    def far_copy(source, target, number):
        return pltpu.make_async_remote_copy(
            src_ref=source,
            dst_ref=target,
            send_sem=far_send.at[number],
            recv_sem=far_recv.at[number],
            device_id=(mate, me),
            device_id_type=MESH,
        )

    ask = far_copy(far_query, far_ask, 0)
    ask.start()

    span = ITEM_PAGES * size
    where = lax.broadcasted_iota(I32, (1, span), 1)
    items = table.shape[1] // ITEM_PAGES

    def score(query, book, row, item, at):
        both = [pages[book[row, item * ITEM_PAGES + k]] for k in range(ITEM_PAGES)]
        for k in range(ITEM_PAGES):
            values[at, k * size : k * size + size, :] = both[k][:, 128:256]
        scores[at] = nt(query, jnp.concatenate([part[:, 0:128] for part in both], 0))

    def gather_up(total, summed, valid, at):
        for part in range(span // 256):
            pieces = []
            for first in (part * 256, part * 256 + 128):
                weight = weigh(scores[at, :, first : first + 128])
                weight = jnp.where(where[:, first : first + 128] < valid, weight, 0.0)
                summed = summed + weight
                pieces.append(weight.astype(BF16))
            total = total + nn(jnp.concatenate(pieces, 1), values[at, part * 256 : part * 256 + 256, :])
        return total, summed

    def run(source, book, length_of, first, last, own, extra=None):
        def body(r, carry):
            query = source[r]
            following = jnp.minimum(r + 1, last - 1)
            length = length_of(r)
            if own:
                new = fresh[pl.ds(pl.multiple_of(r * tree, tree), 128), :]
                mask = masks[r]
                weight = weigh(nt(query, new[:, 0:128])) * jnp.concatenate([mask, mask], 0)
                summed = weight
                total = nn(weight.astype(BF16), new[:, 128:256])
                path[r] = nn(pickers[r].astype(BF16), new[0:tree]).astype(BF16)
            else:
                summed = jnp.zeros((2 * tree, 128), F32)
                total = jnp.zeros((2 * tree, 128), F32)
            for item in range(items):
                if item + 1 < items:
                    score(query, book, r, item + 1, (item + 1) % 2)
                else:
                    score(source[following], book, following, 0, (item + 1) % 2)
                total, summed = gather_up(total, summed, length - item * span, item % 2)
            if own:
                mixed[r] = total
                sums[r] = summed
            else:
                far_reply[r] = total.astype(BF16)
                sums[requests + r] = summed
            if extra is not None:
                extra(r)
            return carry

        score(source[first], book, first, 0, 0)
        lax.fori_loop(first, last, body, 0)

    own_row = lax.broadcasted_iota(I32, (2 * tree, 128), 0)
    own_lane = lax.broadcasted_iota(I32, (2 * tree, 128), 1)

    def settle(r):
        total = mixed[r]
        summed = jnp.sum(sums[r], -1, keepdims=True)
        for j in range(2):
            this = jnp.full((1, 128), pair[0, j], I32) == r
            total = total + jnp.where(this, far_back[j].astype(F32), 0.0)
            spread = jnp.where((own_row == own_lane) & this, row_back[j : j + 1, :], 0.0)
            summed = summed + jnp.sum(spread, -1, keepdims=True)
        final = (total / summed).astype(BF16)
        rows = pl.ds(pl.multiple_of(r * tree, tree), tree)
        out[rows, 0:128] = final[0:tree]
        out[rows, 128:256] = final[tree : 2 * tree]

    run(queries, table, lambda r: lens[r], 0, EARLY, True)
    ask.wait_recv()
    run(far_ask, far_table, lambda r: far_len[r, mate], 0, 2, False)
    for j in range(2):
        summed = jnp.sum(sums[requests + j], -1, keepdims=True)
        row_reply[j : j + 1, :] = jnp.sum(jnp.where(own_row == own_lane, summed, 0.0), 0, keepdims=True)
    replies = far_copy(far_reply, far_back, 1), far_copy(row_reply, row_back, 2)
    for copy in replies:
        copy.start()
    late = 4
    run(queries, table, lambda r: lens[r], EARLY, requests - late, True)
    for copy in replies:
        copy.wait_recv()
    older = (requests - late) // late

    def catch_up(r):
        for number in range(older):
            settle((r - (requests - late)) * older + number)

    run(queries, table, lambda r: lens[r], requests - late, requests, True, catch_up)
    for number in range(late):
        settle(requests - late + number)

    ask.wait_send()
    for copy in replies:
        copy.wait_send()
    for copy in sent:
        copy.wait_send()
    page_all.wait_send()
    table_all.wait_send()


def body(
    mesh, hidden, norm_gain, q_weight, k_weight, v_weight, kv_pages, page_table, cache_len, tree_parent,
    accept_node, pair_slot, far_len, far_table, mig_src, mig_page,
):
    requests, tree = tree_parent.shape
    pool, page_size, _, entry = kv_pages.shape
    page = (page_size, entry)
    tokens, width = hidden.shape
    groups, share = mesh.shape["grp"], mesh.shape["tp"]
    migrations = mig_src.shape[0]
    others = groups - 1
    blocks = norm_gain.shape[0] // 128
    span = ITEM_PAGES * page_size
    rows = 2 * tree
    dma = pltpu.SemaphoreType.DMA
    vmem, smem = pltpu.VMEM, pltpu.SMEM
    out, path = pl.pallas_call(
        functools.partial(kernel, groups, share),
        out_shape=(
            jax.ShapeDtypeStruct((tokens, 256), BF16),
            jax.ShapeDtypeStruct((requests, 8, 256), BF16),
        ),
        in_specs=[pl.BlockSpec(memory_space=pl.ANY)] * 15,
        out_specs=(pl.BlockSpec(memory_space=pltpu.VMEM),) * 2,
        scratch_shapes=[
            smem(page_table.shape, I32),
            smem(cache_len.shape, I32),
            smem(pair_slot.shape, I32),
            smem(accept_node.shape, I32),
            smem(far_len.shape[::-1], I32),
            smem(far_table.shape, I32),
            vmem((1, migrations), I32),
            vmem((1, migrations), I32),
            vmem((blocks, 128), F32),
            vmem(tree_parent.shape, I32),
            vmem((1, 2 * migrations), I32),
            vmem((others, 1, 2 * migrations), I32),
            vmem((groups + 8, 128), I32),
            smem((groups + 8, 128), I32),
            vmem((share * width, 128), F32),
            vmem((share, width, tokens), BF16),
            vmem((share * width, 512), BF16),
            vmem((tokens, 512), F32),
            vmem((8, tokens), F32),
            vmem((width // PARTS, tokens), BF16),
            vmem((tokens, 128), F32),
            vmem((tokens, 128), F32),
            vmem((pool + migrations,) + page, BF16),
            vmem((others * CAP,) + page, BF16),
            vmem((others * CAP,) + page, BF16),
            vmem((requests, tree, 128), F32),
            vmem((requests, 8, tree), F32),
            vmem((requests, rows, 128), BF16),
            vmem((tokens + 128 - tree, 256), BF16),
            vmem((2, rows, span), F32),
            vmem((2, span, 128), BF16),
            vmem((requests, rows, 128), F32),
            vmem((requests + 2, rows, 128), F32),
            vmem((2, rows, 128), BF16),
            vmem((2, rows, 128), BF16),
            vmem((2, rows, 128), BF16),
            vmem((2, rows, 128), BF16),
            vmem((8, 128), F32),
            vmem((8, 128), F32),
            dma((10,)),
            dma((6,)),
            dma((3 * PARTS + 4 * PARTS,)),
            dma((share, PARTS)),
            dma,
            dma,
            dma,
            dma,
            dma((3,)),
            dma((3,)),
        ],
        compiler_params=pltpu.CompilerParams(
            collective_id=0, has_side_effects=True, vmem_limit_bytes=56 << 20
        ),
        name="tree_attention",
    )(
        page_table, cache_len, pair_slot, accept_node, far_len.T, far_table, mig_src[None, :], mig_page[None, :],
        norm_gain.reshape(blocks, 128), tree_parent, hidden.T, kv_pages.reshape((pool,) + page), q_weight,
        k_weight, v_weight,
    )
    return out, path[:, :ACCEPT].reshape(requests * ACCEPT, 1, entry)


def solution(mesh):
    in_specs = (
        P("grp", "tp"),
        P(),
        P(None, "tp"),
        P(None, "tp"),
        P(None, "tp"),
        P("grp", None, "tp", None),
        P("grp", None),
        P("grp"),
        P("grp", None),
        P("grp"),
        P("grp", None),
        P(),
        P("grp", None),
        P("grp"),
        P("grp"),
    )
    out_specs = (P("grp", "tp"), P("grp", "tp", None))
    return jax.shard_map(
        functools.partial(body, mesh), mesh=mesh, in_specs=in_specs, out_specs=out_specs, check_vma=False
    )
```

```python
import functools

import jax
import jax.numpy as jnp
from jax import lax
from jax.experimental import pallas as pl
from jax.experimental.pallas import tpu as pltpu
from jax.sharding import PartitionSpec as P

CAP = 4
ACCEPT = 5
THETA_LOG = 9.210340371976184
PRE = 144.0 ** (-0.5) / 50.0
POST = 50.0 * 1.4426950408889634
PARTS = 4
ITEM_PAGES = 64
EARLY = 4
F32 = jnp.float32
BF16 = jnp.bfloat16
I32 = jnp.int32
MESH = pl.DeviceIdType.MESH


def nt(a, b):
    return lax.dot_general(a, b, (((1,), (1,)), ((), ())), preferred_element_type=F32)


def nn(a, b):
    return lax.dot_general(a, b, (((1,), (0,)), ((), ())), preferred_element_type=F32)


def tn(a, b):
    return lax.dot_general(a, b, (((0,), (0,)), ((), ())), preferred_element_type=F32)


def weigh(scores):
    return jnp.exp2(jnp.tanh(scores * PRE) * POST)


def kernel(
    groups, share,
    table_hbm, lens_hbm, pair_hbm, leaf_hbm, far_len_hbm, far_table_hbm, src_hbm, page_hbm, gain_hbm, parents_hbm,
    hidden, kv_hbm, q_hbm, k_hbm, v_hbm,
    out, path,
    table, lens, pair, leaf, far_len, far_table, own_src, own_page, gain_rows, parents,
    tables, landed, wish, wish_smem, gain, xbuf, weights, acc, squares, xs, cosine, sine, pages, packed, arrived,
    masks, pickers, queries, fresh, scores, values, mixed, sums, far_query, far_ask, far_reply, far_back, row_reply,
    row_back, chain,
    small_sem, local_sem, send_sem, recv_sem, table_send, table_recv, page_send, page_recv, far_send, far_recv, passed,
):
    group = lax.axis_index("grp")
    me = lax.axis_index("tp")
    chips = share // 2
    chip, core = me // 2, me % 2
    right = ((chip + 1) % chips) * 2 + core
    left = ((chip + chips - 1) % chips) * 2 + core
    across = ((chip + 2) % chips) * 2 + core
    sibling = chip * 2 + 1 - core
    others = groups - 1
    mate = group + 1 - 2 * (group % 2)
    width, tokens = hidden.shape
    piece = width // PARTS
    pool, size = kv_hbm.shape[0:2]
    requests, tree = parents.shape
    migrations = own_src.shape[1]

    small = [
        pltpu.make_async_copy(source, target, small_sem.at[number])
        for number, (source, target) in enumerate(
            (
                (src_hbm, own_src),
                (page_hbm, own_page),
                (gain_hbm, gain_rows),
                (parents_hbm, parents),
                (table_hbm, table),
                (lens_hbm, lens),
                (pair_hbm, pair),
                (leaf_hbm, leaf),
                (far_len_hbm, far_len),
                (far_table_hbm, far_table),
            )
        )
    ]
    loads = [
        pltpu.make_async_copy(hidden, xbuf.at[me], local_sem.at[0]),
        pltpu.make_async_copy(kv_hbm, pages.at[pl.ds(0, pool)], local_sem.at[1]),
        pltpu.make_async_copy(q_hbm, weights.at[:, pl.ds(0, 256)], local_sem.at[2]),
        pltpu.make_async_copy(k_hbm, weights.at[:, pl.ds(256, 128)], local_sem.at[3]),
        pltpu.make_async_copy(v_hbm, weights.at[:, pl.ds(384, 128)], local_sem.at[4]),
    ]
    for copy in small[0:2] + loads[1:2] + loads[0:1] + loads[2:] + small[2:]:
        copy.start()

    barrier = pltpu.get_barrier_semaphore()
    for peer in (left // 2, right // 2):
        pl.semaphore_signal(barrier, inc=1, device_id=(group, peer * 2), device_id_type=MESH)

    @pl.when(core == 1)
    def _():
        pl.semaphore_signal(barrier, inc=1, device_id=(group, sibling), device_id_type=MESH)

    def greet(number, carry):
        peer = (group + 1 + number) % groups
        pl.semaphore_signal(barrier, inc=1, device_id=(peer, chip * 2 + 1), device_id_type=MESH)
        return carry

    lax.fori_loop(0, others, greet, 0)

    @pl.when(core == 0)
    def _():
        pl.semaphore_wait(barrier, 5)
        pl.semaphore_signal(passed, inc=1, device_id=(group, sibling), device_id_type=MESH)

    @pl.when(core == 1)
    def _():
        pl.semaphore_wait(passed, 1)

    sent = []

    def send(source, owner, part, peer):
        copy = pltpu.make_async_remote_copy(
            src_ref=source,
            dst_ref=xbuf.at[owner, pl.ds(part * piece, piece)],
            send_sem=send_sem.at[len(sent)],
            recv_sem=recv_sem.at[owner, part],
            device_id=(group, peer),
            device_id_type=MESH,
        )
        copy.start()
        sent.append(copy)

    def own_part(part):
        return hidden.at[pl.ds(part * piece, piece)]

    def held(owner, part):
        return xbuf.at[owner, pl.ds(part * piece, piece)]

    def arrive(owner, part):
        pltpu.make_async_remote_copy(
            src_ref=held(owner, part),
            dst_ref=held(owner, part),
            send_sem=send_sem.at[0],
            recv_sem=recv_sem.at[owner, part],
            device_id=(group, sibling),
            device_id_type=MESH,
        ).wait_recv()

    def table_copy(number):
        return pltpu.make_async_remote_copy(
            src_ref=tables,
            dst_ref=landed.at[number],
            send_sem=table_send,
            recv_sem=table_recv,
            device_id=((group + 1 + number) % groups, me),
            device_id_type=MESH,
        )

    def tell(number, carry):
        table_copy(number).start()
        return carry

    for part in range(PARTS):
        send(own_part(part), me, part, right)
        send(own_part(PARTS - 1 - part), me, PARTS - 1 - part, left)
    for part in range(PARTS):
        send(own_part(part), me, part, sibling)
    small[0].wait()
    small[1].wait()
    tables[:, 0:migrations] = own_src[...]
    tables[:, migrations : 2 * migrations] = own_page[...]

    def blank():
        acc[...] = jnp.zeros_like(acc)
        squares[...] = jnp.zeros_like(squares)
        fresh[...] = jnp.zeros_like(fresh)
        row_reply[...] = jnp.zeros_like(row_reply)

    pages[pl.ds(pool, migrations)] = jnp.zeros((migrations,) + pages.shape[1:], BF16)

    @pl.when(core == 1)
    def _():
        pl.semaphore_wait(barrier, 2 * others)
        pl.semaphore_signal(passed, inc=1, device_id=(group, sibling), device_id_type=MESH)

    @pl.when(core == 0)
    def _():
        pl.semaphore_wait(passed, 1)

    lax.fori_loop(0, others, tell, 0)
    table_all = pltpu.make_async_remote_copy(
        src_ref=landed,
        dst_ref=landed,
        send_sem=table_send,
        recv_sem=table_recv,
        device_id=(mate, me),
        device_id_type=MESH,
    )
    table_all.wait_recv()
    every = jnp.concatenate([landed[number] for number in range(others)] + [tables[...]], 0)
    wide_lane = lax.broadcasted_iota(I32, (groups, 128), 1)

    def before(marks):
        total = marks
        for shift in (1, 2, 4, 8, 16, 32):
            total = total + jnp.where(wide_lane >= shift, pltpu.roll(total, shift, 1), 0)
        return total - marks

    def across_lanes(value):
        for shift in (64, 32, 16, 8, 4, 2, 1):
            value = value + pltpu.roll(value, shift, 1)
        return value

    hits = jnp.where((every == group) & (wide_lane < migrations), 1, 0)
    ranks = before(hits)
    asked = pltpu.roll(every, migrations, 1)
    wanted = jnp.zeros((groups, 128), I32)
    for slot in range(CAP):
        chosen = across_lanes(jnp.where((hits == 1) & (ranks == slot), asked, 0))
        wanted = jnp.where(wide_lane == slot, chosen, wanted)
    mine = jnp.broadcast_to(tables[...], (groups, 128))
    source = lax.broadcasted_iota(I32, (groups, 128), 0)
    marks = jnp.where((source == mine) & (wide_lane < migrations), 1, 0)
    spot = marks * before(marks)
    for shift in (16, 8, 4, 2, 1):
        spot = spot + pltpu.roll(spot, shift, 0)
    spot = ((mine - group + groups) % groups - 1) * CAP + spot
    spot = jnp.minimum(jnp.maximum(spot, 0), others * CAP - 1)
    wish[0:groups, :] = wanted
    wish[groups : groups + 8, :] = jnp.where(wide_lane < migrations, spot, 0)[0:8]
    move = pltpu.make_async_copy(wish, wish_smem, local_sem.at[5])
    move.start()
    move.wait()
    loads[1].wait()

    def page_copy(number):
        return pltpu.make_async_remote_copy(
            src_ref=packed.at[pl.ds(number * CAP, CAP)],
            dst_ref=arrived.at[pl.ds(number * CAP, CAP)],
            send_sem=page_send,
            recv_sem=page_recv,
            device_id=((group + groups - 1 - number) % groups, me),
            device_id_type=MESH,
        )

    for number in range(others):
        for slot in range(CAP):
            packed[number * CAP + slot] = pages[wish_smem[number, slot]]
        page_copy(number).start()
    blank()

    for copy in small[2:]:
        copy.wait()
    blocks = gain_rows.shape[0]
    columns = jnp.transpose(jnp.concatenate([gain_rows[...], jnp.zeros((128 - blocks, 128), F32)], 0))
    for block in range(blocks):
        gain[block * 128 : block * 128 + 128, :] = jnp.broadcast_to(columns[:, block : block + 1], (128, 128))

    def consume(owner, part):
        first = owner * width + part * piece
        total = squares[...]
        for strip in range(piece // 16):
            raw = xbuf[owner, pl.ds(part * piece + strip * 16, 16), :].astype(F32)
            factor = gain[pl.ds(first + strip * 16, 16), :]
            scaled = raw * jnp.concatenate([factor] * (tokens // 128), 1)
            xs[strip * 16 : strip * 16 + 16, :] = scaled.astype(BF16)
            square = raw * raw
            total = total + (square[0:8] + square[8:16])
        squares[...] = total
        block = weights[pl.ds(pl.multiple_of(first, 16), piece), :]
        for m in range(tokens // 256):
            at = slice(m * 256, m * 256 + 256)
            acc[at, :] = acc[at, :] + tn(xs[:, at], block)

    def turn_of(i, low, low_parts, high, high_parts):
        half = len(low_parts)
        step = i % (2 * half)
        is_low = step % 2 == 0
        owner = jnp.where(is_low, low, high)
        at_low = low_parts[0] + (step // 2) * (low_parts[1] - low_parts[0])
        at_high = high_parts[0] + (step // 2) * (high_parts[1] - high_parts[0])
        part = jnp.where(is_low, at_low, at_high)
        return jnp.where(i < 2 * half, owner, owner + 1 - 2 * (owner % 2)), part

    for load in (loads[0], loads[2], loads[3], loads[4]):
        load.wait()

    def take_own(i, carry):
        consume(me, i)
        return carry

    def take_sibling(i, carry):
        arrive(sibling, i)
        consume(sibling, i)
        return carry

    lax.fori_loop(0, PARTS, take_own, 0)
    lax.fori_loop(0, PARTS, take_sibling, 0)

    def take(low, low_parts, high, high_parts):
        half = len(low_parts)

        def direct(i, carry):
            consume(*turn_of(i, low, low_parts, high, high_parts))
            return carry

        def indirect(i, carry):
            owner, part = turn_of(i, low, low_parts, high, high_parts)
            arrive(owner, part)
            consume(owner, part)
            return carry

        lax.fori_loop(0, 2 * half, direct, 0)
        lax.fori_loop(2 * half, 4 * half, indirect, 0)

    ahead, behind = tuple(range(PARTS // 2)), tuple(range(PARTS // 2, PARTS))
    for number in range(PARTS // 2):
        arrive(left, ahead[number])
        send(held(left, ahead[number]), left, ahead[number], right)
        arrive(right, behind[-1 - number])
        send(held(right, behind[-1 - number]), right, behind[-1 - number], left)
    for number in range(PARTS // 2):
        send(held(left, ahead[number]), left, ahead[number], sibling)
        send(held(right, behind[-1 - number]), right, behind[-1 - number], sibling)

    node_row = lax.broadcasted_iota(I32, (tree, tree), 0)
    node_col = lax.broadcasted_iota(I32, (tree, tree), 1)
    eye = jnp.where(node_row == node_col, 1.0, 0.0).astype(BF16)
    levels = lax.broadcasted_iota(I32, (8, tree), 0).astype(F32)
    lane = lax.broadcasted_iota(I32, (1, 128), 1)
    angle = jnp.exp((lane % 64).astype(F32) * (-THETA_LOG * 2.0 / 128.0))
    turn = jnp.where(lane < 64, -1.0, 1.0)
    side = jnp.zeros((tree, 128 - tree), F32)

    def grow(number, carry):
        for half in range(2):
            r = number * 2 + half
            up = jnp.where(node_row == parents[pl.ds(r, 1), :], 1.0, 0.0).astype(BF16) + eye
            for _ in range(2):
                up = jnp.minimum(nn(up, up), 1.0).astype(BF16)
            reached = nt(eye, up)
            masks[r] = jnp.concatenate([reached, side], 1)
            depth_row = jnp.sum(up.astype(F32), 0, keepdims=True) - 1.0
            chosen = jnp.where(node_row == jnp.full((tree, tree), leaf[r], I32), reached, 0.0)
            lineage = jnp.sum(chosen, 0, keepdims=True)
            pickers[r] = jnp.where(depth_row == levels, lineage, 0.0)
            depth = jnp.sum(reached, -1, keepdims=True) - 1.0
            base = jnp.full((1, 128), lens[r], I32)
            for j in range(2):
                base = base + jnp.where(jnp.full((1, 128), pair[0, j], I32) == r, far_len[j, group], 0)
            phase = (base.astype(F32) + depth) * angle
            rows = pl.ds(pl.multiple_of(r * tree, tree), tree)
            cosine[rows, :] = jnp.cos(phase)
            sine[rows, :] = jnp.sin(phase) * turn
        return carry

    take(left, ahead, right, behind[::-1])
    lax.fori_loop(0, requests // 2, grow, 0)
    for number in range(PARTS // 2):
        arrive(left, behind[number])
        send(held(left, behind[number]), left, behind[number], sibling)
        arrive(right, ahead[-1 - number])
        send(held(right, ahead[-1 - number]), right, ahead[-1 - number], sibling)
    take(left, behind, right, ahead[::-1])

    page_all = pltpu.make_async_remote_copy(
        src_ref=packed,
        dst_ref=arrived,
        send_sem=page_send,
        recv_sem=page_recv,
        device_id=(mate, me),
        device_id_type=MESH,
    )
    page_all.wait_recv()
    for number in range(migrations):
        pages[pool + number] = arrived[wish_smem[groups, number]]

    for number in range(PARTS // 2):
        arrive(across, ahead[number])
        send(held(across, ahead[number]), across, ahead[number], sibling)
        arrive(across, behind[-1 - number])
        send(held(across, behind[-1 - number]), across, behind[-1 - number], sibling)
    take(across, ahead, across, behind[::-1])

    mean = lax.dot_general(
        squares[...], jnp.full((8, 128), 1.0 / (share * width), F32), (((0,), (0,)), ((), ())),
        precision=lax.Precision.HIGHEST, preferred_element_type=F32,
    )
    scale = lax.rsqrt(mean + 1e-06)
    cosine[...] = cosine[...] * scale
    sine[...] = sine[...] * scale
    fresh[0:tokens, 128:256] = (acc[:, 384:512] * scale).astype(BF16)

    def turned(rows, at):
        value = acc[rows, at : at + 128]
        return (value * cosine[rows, :] + pltpu.roll(value, 64, 1) * sine[rows, :]).astype(BF16)

    def finish(number, carry):
        for half in range(2):
            r = number * 2 + half
            rows = pl.ds(pl.multiple_of(r * tree, tree), tree)
            fresh[rows, 0:128] = turned(rows, 256)
            queries[r, 0:tree, :] = turned(rows, 0)
            queries[r, tree : 2 * tree, :] = turned(rows, 128)
        return carry

    lax.fori_loop(0, requests // 2, finish, 0)
    for j in range(2):
        far_query[j] = queries[pair[0, j]]

    def far_copy(source, target, number):
        return pltpu.make_async_remote_copy(
            src_ref=source,
            dst_ref=target,
            send_sem=far_send.at[number],
            recv_sem=far_recv.at[number],
            device_id=(mate, me),
            device_id_type=MESH,
        )

    ask = far_copy(far_query, far_ask, 0)
    ask.start()

    span = ITEM_PAGES * size
    where = lax.broadcasted_iota(I32, (1, span), 1)
    items = table.shape[1] // ITEM_PAGES

    def score(query, book, row, item, at):
        both = [pages[book[row, item * ITEM_PAGES + k]] for k in range(ITEM_PAGES)]
        for k in range(ITEM_PAGES):
            values[at, k * size : k * size + size, :] = both[k][:, 128:256]
        scores[at] = nt(query, jnp.concatenate([part[:, 0:128] for part in both], 0))

    def gather_up(total, summed, valid, at):
        for part in range(span // 256):
            pieces = []
            for first in (part * 256, part * 256 + 128):
                weight = weigh(scores[at, :, first : first + 128])
                weight = jnp.where(where[:, first : first + 128] < valid, weight, 0.0)
                summed = summed + weight
                pieces.append(weight.astype(BF16))
            total = total + nn(jnp.concatenate(pieces, 1), values[at, part * 256 : part * 256 + 256, :])
        return total, summed

    def run(source, book, length_of, first, last, own, extra=None):
        def body(r, carry):
            query = source[r]
            following = jnp.minimum(r + 1, last - 1)
            length = length_of(r)
            if own:
                new = fresh[pl.ds(pl.multiple_of(r * tree, tree), 128), :]
                mask = masks[r]
                weight = weigh(nt(query, new[:, 0:128])) * jnp.concatenate([mask, mask], 0)
                summed = weight
                total = nn(weight.astype(BF16), new[:, 128:256])
                chain[pl.ds(pl.multiple_of(r * 8, 8), 8), :] = nn(pickers[r].astype(BF16), new[0:tree])
            else:
                summed = jnp.zeros((2 * tree, 128), F32)
                total = jnp.zeros((2 * tree, 128), F32)
            for item in range(items):
                if item + 1 < items:
                    score(query, book, r, item + 1, (item + 1) % 2)
                else:
                    score(source[following], book, following, 0, (item + 1) % 2)
                total, summed = gather_up(total, summed, length - item * span, item % 2)
            if own:
                mixed[r] = total
                sums[r] = summed
            else:
                far_reply[r] = total.astype(BF16)
                sums[requests + r] = summed
            if extra is not None:
                extra(r)
            return carry

        score(source[first], book, first, 0, 0)
        lax.fori_loop(first, last, body, 0)

    own_row = lax.broadcasted_iota(I32, (2 * tree, 128), 0)
    own_lane = lax.broadcasted_iota(I32, (2 * tree, 128), 1)

    def settle(r):
        total = mixed[r]
        summed = jnp.sum(sums[r], -1, keepdims=True)
        for j in range(2):
            this = jnp.full((1, 128), pair[0, j], I32) == r
            total = total + jnp.where(this, far_back[j].astype(F32), 0.0)
            spread = jnp.where((own_row == own_lane) & this, row_back[j : j + 1, :], 0.0)
            summed = summed + jnp.sum(spread, -1, keepdims=True)
        final = (total / summed).astype(BF16)
        rows = pl.ds(pl.multiple_of(r * tree, tree), tree)
        out[rows, 0:128] = final[0:tree]
        out[rows, 128:256] = final[tree : 2 * tree]

    run(queries, table, lambda r: lens[r], 0, EARLY, True)
    ask.wait_recv()
    run(far_ask, far_table, lambda r: far_len[r, mate], 0, 2, False)
    for j in range(2):
        summed = jnp.sum(sums[requests + j], -1, keepdims=True)
        row_reply[j : j + 1, :] = jnp.sum(jnp.where(own_row == own_lane, summed, 0.0), 0, keepdims=True)
    replies = far_copy(far_reply, far_back, 1), far_copy(row_reply, row_back, 2)
    for copy in replies:
        copy.start()
    late = 4
    run(queries, table, lambda r: lens[r], EARLY, requests - late, True)
    for copy in replies:
        copy.wait_recv()
    older = (requests - late) // late

    def catch_up(r):
        for number in range(older):
            settle((r - (requests - late)) * older + number)

    run(queries, table, lambda r: lens[r], requests - late, requests, True, catch_up)
    row_of = lax.broadcasted_iota(I32, path.shape[0:1] + (8 * requests,), 0)
    place = lax.broadcasted_iota(I32, path.shape[0:1] + (8 * requests,), 1)
    compact = jnp.where(place == row_of // ACCEPT * 8 + row_of % ACCEPT, 1.0, 0.0).astype(BF16)
    path[...] = nn(compact, chain[...].astype(BF16)).astype(BF16)
    for number in range(late):
        settle(requests - late + number)

    ask.wait_send()
    for copy in replies:
        copy.wait_send()
    for copy in sent:
        copy.wait_send()
    page_all.wait_send()
    table_all.wait_send()


def deliver(out, path, out_final, path_final, sems):
    copies = (
        pltpu.make_async_copy(out, out_final, sems.at[0]),
        pltpu.make_async_copy(path, path_final, sems.at[1]),
    )
    for copy in copies:
        copy.start()
    for copy in copies:
        copy.wait()


def body(
    mesh, hidden, norm_gain, q_weight, k_weight, v_weight, kv_pages, page_table, cache_len, tree_parent,
    accept_node, pair_slot, far_len, far_table, mig_src, mig_page,
):
    requests, tree = tree_parent.shape
    pool, page_size, _, entry = kv_pages.shape
    page = (page_size, entry)
    tokens, width = hidden.shape
    groups, share = mesh.shape["grp"], mesh.shape["tp"]
    migrations = mig_src.shape[0]
    others = groups - 1
    blocks = norm_gain.shape[0] // 128
    span = ITEM_PAGES * page_size
    rows = 2 * tree
    dma = pltpu.SemaphoreType.DMA
    vmem, smem = pltpu.VMEM, pltpu.SMEM
    out, path = pl.pallas_call(
        functools.partial(kernel, groups, share),
        out_shape=(
            jax.ShapeDtypeStruct((tokens, 256), BF16),
            jax.ShapeDtypeStruct((requests * ACCEPT, 256), BF16),
        ),
        in_specs=[pl.BlockSpec(memory_space=pl.ANY)] * 15,
        out_specs=(pl.BlockSpec(memory_space=pltpu.VMEM),) * 2,
        scratch_shapes=[
            smem(page_table.shape, I32),
            smem(cache_len.shape, I32),
            smem(pair_slot.shape, I32),
            smem(accept_node.shape, I32),
            smem(far_len.shape[::-1], I32),
            smem(far_table.shape, I32),
            vmem((1, migrations), I32),
            vmem((1, migrations), I32),
            vmem((blocks, 128), F32),
            vmem(tree_parent.shape, I32),
            vmem((1, 2 * migrations), I32),
            vmem((others, 1, 2 * migrations), I32),
            vmem((groups + 8, 128), I32),
            smem((groups + 8, 128), I32),
            vmem((share * width, 128), F32),
            vmem((share, width, tokens), BF16),
            vmem((share * width, 512), BF16),
            vmem((tokens, 512), F32),
            vmem((8, tokens), F32),
            vmem((width // PARTS, tokens), BF16),
            vmem((tokens, 128), F32),
            vmem((tokens, 128), F32),
            vmem((pool + migrations,) + page, BF16),
            vmem((others * CAP,) + page, BF16),
            vmem((others * CAP,) + page, BF16),
            vmem((requests, tree, 128), F32),
            vmem((requests, 8, tree), F32),
            vmem((requests, rows, 128), BF16),
            vmem((tokens + 128 - tree, 256), BF16),
            vmem((2, rows, span), F32),
            vmem((2, span, 128), BF16),
            vmem((requests, rows, 128), F32),
            vmem((requests + 2, rows, 128), F32),
            vmem((2, rows, 128), BF16),
            vmem((2, rows, 128), BF16),
            vmem((2, rows, 128), BF16),
            vmem((2, rows, 128), BF16),
            vmem((8, 128), F32),
            vmem((8, 128), F32),
            vmem((8 * requests, 256), F32),
            dma((10,)),
            dma((6,)),
            dma((3 * PARTS + 4 * PARTS,)),
            dma((share, PARTS)),
            dma,
            dma,
            dma,
            dma,
            dma((3,)),
            dma((3,)),
            pltpu.SemaphoreType.REGULAR,
        ],
        compiler_params=pltpu.CompilerParams(
            collective_id=0, has_side_effects=True, vmem_limit_bytes=56 << 20
        ),
        name="tree_attention",
    )(
        page_table, cache_len, pair_slot, accept_node, far_len.T, far_table, mig_src[None, :], mig_page[None, :],
        norm_gain.reshape(blocks, 128), tree_parent, hidden.T, kv_pages.reshape((pool,) + page), q_weight,
        k_weight, v_weight,
    )
    out, path = pl.pallas_call(
        deliver,
        out_shape=(
            jax.ShapeDtypeStruct(out.shape, BF16),
            jax.ShapeDtypeStruct(path.shape, BF16),
        ),
        in_specs=[pl.BlockSpec(memory_space=pltpu.VMEM)] * 2,
        out_specs=(pl.BlockSpec(memory_space=pl.ANY),) * 2,
        scratch_shapes=[dma((2,))],
        name="deliver",
    )(out, path)
    return out, path[:, None, :]


def solution(mesh):
    in_specs = (
        P("grp", "tp"),
        P(),
        P(None, "tp"),
        P(None, "tp"),
        P(None, "tp"),
        P("grp", None, "tp", None),
        P("grp", None),
        P("grp"),
        P("grp", None),
        P("grp"),
        P("grp", None),
        P(),
        P("grp", None),
        P("grp"),
        P("grp"),
    )
    out_specs = (P("grp", "tp"), P("grp", "tp", None))
    return jax.shard_map(
        functools.partial(body, mesh), mesh=mesh, in_specs=in_specs, out_specs=out_specs, check_vma=False
    )
```

```python
import functools

import jax
import jax.numpy as jnp
from jax import lax
from jax.experimental import pallas as pl
from jax.experimental.pallas import tpu as pltpu
from jax.sharding import PartitionSpec as P

CAP = 4
ACCEPT = 5
THETA_LOG = 9.210340371976184
PRE = 144.0 ** (-0.5) / 50.0
POST = 50.0 * 1.4426950408889634
PARTS = 4
ITEM_PAGES = 64
EARLY = 4
F32 = jnp.float32
BF16 = jnp.bfloat16
I32 = jnp.int32
MESH = pl.DeviceIdType.MESH


def nt(a, b):
    return lax.dot_general(a, b, (((1,), (1,)), ((), ())), preferred_element_type=F32)


def nn(a, b):
    return lax.dot_general(a, b, (((1,), (0,)), ((), ())), preferred_element_type=F32)


def tn(a, b):
    return lax.dot_general(a, b, (((0,), (0,)), ((), ())), preferred_element_type=F32)


def weigh(scores):
    return jnp.exp2(jnp.tanh(scores * PRE) * POST)


def kernel(
    groups, share,
    table_hbm, lens_hbm, pair_hbm, leaf_hbm, far_len_hbm, far_table_hbm, src_hbm, page_hbm, gain_hbm, parents_hbm,
    hidden, kv_hbm, q_hbm, k_hbm, v_hbm,
    out, path,
    table, lens, pair, leaf, far_len, far_table, own_src, own_page, gain_rows, parents,
    tables, landed, wish, wish_smem, gain, xbuf, weights, acc, squares, xs, cosine, sine, pages, packed, arrived,
    masks, pickers, queries, fresh, scores, values, mixed, sums, far_query, far_ask, far_reply, far_back, row_reply,
    row_back, chain,
    small_sem, local_sem, send_sem, recv_sem, table_send, table_recv, page_send, page_recv, far_send, far_recv, passed,
):
    group = lax.axis_index("grp")
    me = lax.axis_index("tp")
    chips = share // 2
    chip, core = me // 2, me % 2
    right = ((chip + 1) % chips) * 2 + core
    left = ((chip + chips - 1) % chips) * 2 + core
    across = ((chip + 2) % chips) * 2 + core
    sibling = chip * 2 + 1 - core
    others = groups - 1
    mate = group + 1 - 2 * (group % 2)
    width, tokens = hidden.shape
    piece = width // PARTS
    pool, size = kv_hbm.shape[0:2]
    requests, tree = parents.shape
    migrations = own_src.shape[1]

    small = [
        pltpu.make_async_copy(source, target, small_sem.at[number])
        for number, (source, target) in enumerate(
            (
                (src_hbm, own_src),
                (page_hbm, own_page),
                (gain_hbm, gain_rows),
                (parents_hbm, parents),
                (table_hbm, table),
                (lens_hbm, lens),
                (pair_hbm, pair),
                (leaf_hbm, leaf),
                (far_len_hbm, far_len),
                (far_table_hbm, far_table),
            )
        )
    ]
    loads = [
        pltpu.make_async_copy(hidden, xbuf.at[me], local_sem.at[0]),
        pltpu.make_async_copy(kv_hbm, pages.at[pl.ds(0, pool)], local_sem.at[1]),
        pltpu.make_async_copy(q_hbm, weights.at[:, pl.ds(0, 256)], local_sem.at[2]),
        pltpu.make_async_copy(k_hbm, weights.at[:, pl.ds(256, 128)], local_sem.at[3]),
        pltpu.make_async_copy(v_hbm, weights.at[:, pl.ds(384, 128)], local_sem.at[4]),
    ]
    for copy in small[0:2] + loads[1:2] + loads[0:1] + loads[2:] + small[2:]:
        copy.start()

    barrier = pltpu.get_barrier_semaphore()
    for peer in (left // 2, right // 2):
        pl.semaphore_signal(barrier, inc=1, device_id=(group, peer * 2), device_id_type=MESH)

    @pl.when(core == 1)
    def _():
        pl.semaphore_signal(barrier, inc=1, device_id=(group, sibling), device_id_type=MESH)

    def ahead_of(number):
        peer = group + 1 + number
        return jnp.where(peer >= groups, peer - groups, peer)

    def behind_of(number):
        peer = group - 1 - number
        return jnp.where(peer < 0, peer + groups, peer)

    def greet():
        for number in range(others):
            peer = (ahead_of(number), chip * 2 + 1)
            pl.semaphore_signal(barrier, inc=1, device_id=peer, device_id_type=MESH)

    greet()

    @pl.when(core == 0)
    def _():
        pl.semaphore_wait(barrier, 5)
        pl.semaphore_signal(passed, inc=1, device_id=(group, sibling), device_id_type=MESH)

    @pl.when(core == 1)
    def _():
        pl.semaphore_wait(passed, 1)

    sent = []

    def send(source, owner, part, peer):
        copy = pltpu.make_async_remote_copy(
            src_ref=source,
            dst_ref=xbuf.at[owner, pl.ds(part * piece, piece)],
            send_sem=send_sem.at[len(sent)],
            recv_sem=recv_sem.at[owner, part],
            device_id=(group, peer),
            device_id_type=MESH,
        )
        copy.start()
        sent.append(copy)

    def own_part(part):
        return hidden.at[pl.ds(part * piece, piece)]

    def held(owner, part):
        return xbuf.at[owner, pl.ds(part * piece, piece)]

    def arrive(owner, part):
        pltpu.make_async_remote_copy(
            src_ref=held(owner, part),
            dst_ref=held(owner, part),
            send_sem=send_sem.at[0],
            recv_sem=recv_sem.at[owner, part],
            device_id=(group, sibling),
            device_id_type=MESH,
        ).wait_recv()

    def table_copy(number):
        return pltpu.make_async_remote_copy(
            src_ref=tables,
            dst_ref=landed.at[number],
            send_sem=table_send,
            recv_sem=table_recv,
            device_id=(ahead_of(number), me),
            device_id_type=MESH,
        )

    for part in range(PARTS):
        send(own_part(part), me, part, right)
        send(own_part(PARTS - 1 - part), me, PARTS - 1 - part, left)
    for part in range(PARTS):
        send(own_part(part), me, part, sibling)
    small[0].wait()
    small[1].wait()
    tables[:, 0:migrations] = own_src[...]
    tables[:, migrations : 2 * migrations] = own_page[...]

    def blank():
        acc[...] = jnp.zeros_like(acc)
        squares[...] = jnp.zeros_like(squares)
        fresh[...] = jnp.zeros_like(fresh)
        row_reply[...] = jnp.zeros_like(row_reply)

    pages[pl.ds(pool, migrations)] = jnp.zeros((migrations,) + pages.shape[1:], BF16)

    @pl.when(core == 1)
    def _():
        pl.semaphore_wait(barrier, 2 * others)
        pl.semaphore_signal(passed, inc=1, device_id=(group, sibling), device_id_type=MESH)

    @pl.when(core == 0)
    def _():
        pl.semaphore_wait(passed, 1)

    for number in range(others):
        table_copy(number).start()
    table_all = pltpu.make_async_remote_copy(
        src_ref=landed,
        dst_ref=landed,
        send_sem=table_send,
        recv_sem=table_recv,
        device_id=(mate, me),
        device_id_type=MESH,
    )
    table_all.wait_recv()
    every = jnp.concatenate([landed[number] for number in range(others)] + [tables[...]], 0)
    wide_lane = lax.broadcasted_iota(I32, (groups, 128), 1)

    def before(marks):
        total = marks
        for shift in (1, 2, 4, 8, 16, 32):
            total = total + jnp.where(wide_lane >= shift, pltpu.roll(total, shift, 1), 0)
        return total - marks

    def across_lanes(value):
        for shift in (64, 32, 16, 8, 4, 2, 1):
            value = value + pltpu.roll(value, shift, 1)
        return value

    hits = jnp.where((every == group) & (wide_lane < migrations), 1, 0)
    ranks = before(hits)
    asked = pltpu.roll(every, migrations, 1)
    wanted = jnp.zeros((groups, 128), I32)
    for slot in range(CAP):
        chosen = across_lanes(jnp.where((hits == 1) & (ranks == slot), asked, 0))
        wanted = jnp.where(wide_lane == slot, chosen, wanted)
    mine = jnp.broadcast_to(tables[...], (groups, 128))
    source = lax.broadcasted_iota(I32, (groups, 128), 0)
    marks = jnp.where((source == mine) & (wide_lane < migrations), 1, 0)
    spot = marks * before(marks)
    for shift in (16, 8, 4, 2, 1):
        spot = spot + pltpu.roll(spot, shift, 0)
    spot = ((mine - group + groups) % groups - 1) * CAP + spot
    spot = jnp.minimum(jnp.maximum(spot, 0), others * CAP - 1)
    wish[0:groups, :] = wanted
    wish[groups : groups + 8, :] = jnp.where(wide_lane < migrations, spot, 0)[0:8]
    move = pltpu.make_async_copy(wish, wish_smem, local_sem.at[5])
    move.start()
    move.wait()
    loads[1].wait()

    def page_copy(number):
        return pltpu.make_async_remote_copy(
            src_ref=packed.at[pl.ds(number * CAP, CAP)],
            dst_ref=arrived.at[pl.ds(number * CAP, CAP)],
            send_sem=page_send,
            recv_sem=page_recv,
            device_id=(behind_of(number), me),
            device_id_type=MESH,
        )

    for number in range(others):
        for slot in range(CAP):
            packed[number * CAP + slot] = pages[wish_smem[number, slot]]
        page_copy(number).start()
    blank()

    for copy in small[2:]:
        copy.wait()
    blocks = gain_rows.shape[0]
    columns = jnp.transpose(jnp.concatenate([gain_rows[...], jnp.zeros((128 - blocks, 128), F32)], 0))
    for block in range(blocks):
        gain[block * 128 : block * 128 + 128, :] = jnp.broadcast_to(columns[:, block : block + 1], (128, 128))

    def consume(owner, part):
        first = owner * width + part * piece
        total = squares[...]
        for strip in range(piece // 16):
            raw = xbuf[owner, pl.ds(part * piece + strip * 16, 16), :].astype(F32)
            factor = gain[pl.ds(first + strip * 16, 16), :]
            scaled = raw * jnp.concatenate([factor] * (tokens // 128), 1)
            xs[strip * 16 : strip * 16 + 16, :] = scaled.astype(BF16)
            square = raw * raw
            total = total + (square[0:8] + square[8:16])
        squares[...] = total
        block = weights[pl.ds(pl.multiple_of(first, 16), piece), :]
        for m in range(tokens // 256):
            at = slice(m * 256, m * 256 + 256)
            acc[at, :] = acc[at, :] + tn(xs[:, at], block)

    def turn_of(i, low, low_parts, high, high_parts):
        half = len(low_parts)
        step = i % (2 * half)
        is_low = step % 2 == 0
        owner = jnp.where(is_low, low, high)
        at_low = low_parts[0] + (step // 2) * (low_parts[1] - low_parts[0])
        at_high = high_parts[0] + (step // 2) * (high_parts[1] - high_parts[0])
        part = jnp.where(is_low, at_low, at_high)
        return jnp.where(i < 2 * half, owner, owner + 1 - 2 * (owner % 2)), part

    for load in (loads[0], loads[2], loads[3], loads[4]):
        load.wait()

    def take_own(i, carry):
        consume(me, i)
        return carry

    def take_sibling(i, carry):
        arrive(sibling, i)
        consume(sibling, i)
        return carry

    lax.fori_loop(0, PARTS, take_own, 0)
    lax.fori_loop(0, PARTS, take_sibling, 0)

    def take(low, low_parts, high, high_parts):
        half = len(low_parts)

        def direct(i, carry):
            consume(*turn_of(i, low, low_parts, high, high_parts))
            return carry

        def indirect(i, carry):
            owner, part = turn_of(i, low, low_parts, high, high_parts)
            arrive(owner, part)
            consume(owner, part)
            return carry

        lax.fori_loop(0, 2 * half, direct, 0)
        lax.fori_loop(2 * half, 4 * half, indirect, 0)

    ahead, behind = tuple(range(PARTS // 2)), tuple(range(PARTS // 2, PARTS))
    for number in range(PARTS // 2):
        arrive(left, ahead[number])
        send(held(left, ahead[number]), left, ahead[number], right)
        arrive(right, behind[-1 - number])
        send(held(right, behind[-1 - number]), right, behind[-1 - number], left)
    for number in range(PARTS // 2):
        send(held(left, ahead[number]), left, ahead[number], sibling)
        send(held(right, behind[-1 - number]), right, behind[-1 - number], sibling)

    node_row = lax.broadcasted_iota(I32, (tree, tree), 0)
    node_col = lax.broadcasted_iota(I32, (tree, tree), 1)
    eye = jnp.where(node_row == node_col, 1.0, 0.0).astype(BF16)
    levels = lax.broadcasted_iota(I32, (8, tree), 0).astype(F32)
    lane = lax.broadcasted_iota(I32, (1, 128), 1)
    angle = jnp.exp((lane % 64).astype(F32) * (-THETA_LOG * 2.0 / 128.0))
    turn = jnp.where(lane < 64, -1.0, 1.0)
    side = jnp.zeros((tree, 128 - tree), F32)

    def grow(number, carry):
        for half in range(2):
            r = number * 2 + half
            up = jnp.where(node_row == parents[pl.ds(r, 1), :], 1.0, 0.0).astype(BF16) + eye
            for _ in range(2):
                up = jnp.minimum(nn(up, up), 1.0).astype(BF16)
            reached = nt(eye, up)
            masks[r] = jnp.concatenate([reached, side], 1)
            depth_row = jnp.sum(up.astype(F32), 0, keepdims=True) - 1.0
            chosen = jnp.where(node_row == jnp.full((tree, tree), leaf[r], I32), reached, 0.0)
            lineage = jnp.sum(chosen, 0, keepdims=True)
            pickers[r] = jnp.where(depth_row == levels, lineage, 0.0)
            depth = jnp.sum(reached, -1, keepdims=True) - 1.0
            base = jnp.full((1, 128), lens[r], I32)
            for j in range(2):
                base = base + jnp.where(jnp.full((1, 128), pair[0, j], I32) == r, far_len[j, group], 0)
            phase = (base.astype(F32) + depth) * angle
            rows = pl.ds(pl.multiple_of(r * tree, tree), tree)
            cosine[rows, :] = jnp.cos(phase)
            sine[rows, :] = jnp.sin(phase) * turn
        return carry

    take(left, ahead, right, behind[::-1])
    lax.fori_loop(0, requests // 2, grow, 0)
    for number in range(PARTS // 2):
        arrive(left, behind[number])
        send(held(left, behind[number]), left, behind[number], sibling)
        arrive(right, ahead[-1 - number])
        send(held(right, ahead[-1 - number]), right, ahead[-1 - number], sibling)
    take(left, behind, right, ahead[::-1])

    page_all = pltpu.make_async_remote_copy(
        src_ref=packed,
        dst_ref=arrived,
        send_sem=page_send,
        recv_sem=page_recv,
        device_id=(mate, me),
        device_id_type=MESH,
    )

    for number in range(PARTS // 2):
        arrive(across, ahead[number])
        send(held(across, ahead[number]), across, ahead[number], sibling)
        arrive(across, behind[-1 - number])
        send(held(across, behind[-1 - number]), across, behind[-1 - number], sibling)
    take(across, ahead, across, behind[::-1])

    mean = lax.dot_general(
        squares[...], jnp.full((8, 128), 1.0 / (share * width), F32), (((0,), (0,)), ((), ())),
        precision=lax.Precision.HIGHEST, preferred_element_type=F32,
    )
    scale = lax.rsqrt(mean + 1e-06)
    cosine[...] = cosine[...] * scale
    sine[...] = sine[...] * scale
    fresh[0:tokens, 128:256] = (acc[:, 384:512] * scale).astype(BF16)

    def turned(rows, at):
        value = acc[rows, at : at + 128]
        return (value * cosine[rows, :] + pltpu.roll(value, 64, 1) * sine[rows, :]).astype(BF16)

    def finish(number, carry):
        for half in range(2):
            r = number * 2 + half
            rows = pl.ds(pl.multiple_of(r * tree, tree), tree)
            fresh[rows, 0:128] = turned(rows, 256)
            queries[r, 0:tree, :] = turned(rows, 0)
            queries[r, tree : 2 * tree, :] = turned(rows, 128)
        return carry

    lax.fori_loop(0, requests // 2, finish, 0)
    for j in range(2):
        far_query[j] = queries[pair[0, j]]

    def far_copy(source, target, number):
        return pltpu.make_async_remote_copy(
            src_ref=source,
            dst_ref=target,
            send_sem=far_send.at[number],
            recv_sem=far_recv.at[number],
            device_id=(mate, me),
            device_id_type=MESH,
        )

    ask = far_copy(far_query, far_ask, 0)
    ask.start()
    page_all.wait_recv()
    for number in range(migrations):
        pages[pool + number] = arrived[wish_smem[groups, number]]

    span = ITEM_PAGES * size
    where = lax.broadcasted_iota(I32, (1, span), 1)
    items = table.shape[1] // ITEM_PAGES

    def score(query, book, row, item, at):
        both = [pages[book[row, item * ITEM_PAGES + k]] for k in range(ITEM_PAGES)]
        for k in range(ITEM_PAGES):
            values[at, k * size : k * size + size, :] = both[k][:, 128:256]
        scores[at] = nt(query, jnp.concatenate([part[:, 0:128] for part in both], 0))

    def gather_up(total, summed, valid, at):
        for part in range(span // 256):
            pieces = []
            for first in (part * 256, part * 256 + 128):
                weight = weigh(scores[at, :, first : first + 128])
                weight = jnp.where(where[:, first : first + 128] < valid, weight, 0.0)
                summed = summed + weight
                pieces.append(weight.astype(BF16))
            total = total + nn(jnp.concatenate(pieces, 1), values[at, part * 256 : part * 256 + 256, :])
        return total, summed

    def run(source, book, length_of, first, last, own, extra=None):
        def body(r, carry):
            query = source[r]
            following = jnp.minimum(r + 1, last - 1)
            length = length_of(r)
            if own:
                new = fresh[pl.ds(pl.multiple_of(r * tree, tree), 128), :]
                mask = masks[r]
                weight = weigh(nt(query, new[:, 0:128])) * jnp.concatenate([mask, mask], 0)
                summed = weight
                total = nn(weight.astype(BF16), new[:, 128:256])
                chain[pl.ds(pl.multiple_of(r * 8, 8), 8), :] = nn(pickers[r].astype(BF16), new[0:tree])
            else:
                summed = jnp.zeros((2 * tree, 128), F32)
                total = jnp.zeros((2 * tree, 128), F32)
            for item in range(items):
                if item + 1 < items:
                    score(query, book, r, item + 1, (item + 1) % 2)
                else:
                    score(source[following], book, following, 0, (item + 1) % 2)
                total, summed = gather_up(total, summed, length - item * span, item % 2)
            if own:
                mixed[r] = total
                sums[r] = summed
            else:
                far_reply[r] = total.astype(BF16)
                sums[requests + r] = summed
            if extra is not None:
                extra(r)
            return carry

        score(source[first], book, first, 0, 0)
        lax.fori_loop(first, last, body, 0)

    own_row = lax.broadcasted_iota(I32, (2 * tree, 128), 0)
    own_lane = lax.broadcasted_iota(I32, (2 * tree, 128), 1)

    def settle(r):
        total = mixed[r]
        summed = jnp.sum(sums[r], -1, keepdims=True)
        for j in range(2):
            this = jnp.full((1, 128), pair[0, j], I32) == r
            total = total + jnp.where(this, far_back[j].astype(F32), 0.0)
            spread = jnp.where((own_row == own_lane) & this, row_back[j : j + 1, :], 0.0)
            summed = summed + jnp.sum(spread, -1, keepdims=True)
        final = (total / summed).astype(BF16)
        rows = pl.ds(pl.multiple_of(r * tree, tree), tree)
        out[rows, 0:128] = final[0:tree]
        out[rows, 128:256] = final[tree : 2 * tree]

    run(queries, table, lambda r: lens[r], 0, EARLY, True)
    ask.wait_recv()
    run(far_ask, far_table, lambda r: far_len[r, mate], 0, 2, False)
    for j in range(2):
        summed = jnp.sum(sums[requests + j], -1, keepdims=True)
        row_reply[j : j + 1, :] = jnp.sum(jnp.where(own_row == own_lane, summed, 0.0), 0, keepdims=True)
    replies = far_copy(far_reply, far_back, 1), far_copy(row_reply, row_back, 2)
    for copy in replies:
        copy.start()
    late = 4
    run(queries, table, lambda r: lens[r], EARLY, requests - late, True)
    for copy in replies:
        copy.wait_recv()
    older = (requests - late) // late

    def catch_up(r):
        for number in range(older):
            settle((r - (requests - late)) * older + number)

    run(queries, table, lambda r: lens[r], requests - late, requests, True, catch_up)
    row_of = lax.broadcasted_iota(I32, path.shape[0:1] + (8 * requests,), 0)
    place = lax.broadcasted_iota(I32, path.shape[0:1] + (8 * requests,), 1)
    compact = jnp.where(place == row_of // ACCEPT * 8 + row_of % ACCEPT, 1.0, 0.0).astype(BF16)
    path[...] = nn(compact, chain[...].astype(BF16)).astype(BF16)
    for number in range(late):
        settle(requests - late + number)

    ask.wait_send()
    for copy in replies:
        copy.wait_send()
    for copy in sent:
        copy.wait_send()
    page_all.wait_send()
    table_all.wait_send()


def deliver(out, path, out_final, path_final, sems):
    copies = (
        pltpu.make_async_copy(out, out_final, sems.at[0]),
        pltpu.make_async_copy(path, path_final, sems.at[1]),
    )
    for copy in copies:
        copy.start()
    for copy in copies:
        copy.wait()


def body(
    mesh, hidden, norm_gain, q_weight, k_weight, v_weight, kv_pages, page_table, cache_len, tree_parent,
    accept_node, pair_slot, far_len, far_table, mig_src, mig_page,
):
    requests, tree = tree_parent.shape
    pool, page_size, _, entry = kv_pages.shape
    page = (page_size, entry)
    tokens, width = hidden.shape
    groups, share = mesh.shape["grp"], mesh.shape["tp"]
    migrations = mig_src.shape[0]
    others = groups - 1
    blocks = norm_gain.shape[0] // 128
    span = ITEM_PAGES * page_size
    rows = 2 * tree
    dma = pltpu.SemaphoreType.DMA
    vmem, smem = pltpu.VMEM, pltpu.SMEM
    out, path = pl.pallas_call(
        functools.partial(kernel, groups, share),
        out_shape=(
            jax.ShapeDtypeStruct((tokens, 256), BF16),
            jax.ShapeDtypeStruct((requests * ACCEPT, 256), BF16),
        ),
        in_specs=[pl.BlockSpec(memory_space=pl.ANY)] * 15,
        out_specs=(pl.BlockSpec(memory_space=pltpu.VMEM),) * 2,
        scratch_shapes=[
            smem(page_table.shape, I32),
            smem(cache_len.shape, I32),
            smem(pair_slot.shape, I32),
            smem(accept_node.shape, I32),
            smem(far_len.shape[::-1], I32),
            smem(far_table.shape, I32),
            vmem((1, migrations), I32),
            vmem((1, migrations), I32),
            vmem((blocks, 128), F32),
            vmem(tree_parent.shape, I32),
            vmem((1, 2 * migrations), I32),
            vmem((others, 1, 2 * migrations), I32),
            vmem((groups + 8, 128), I32),
            smem((groups + 8, 128), I32),
            vmem((share * width, 128), F32),
            vmem((share, width, tokens), BF16),
            vmem((share * width, 512), BF16),
            vmem((tokens, 512), F32),
            vmem((8, tokens), F32),
            vmem((width // PARTS, tokens), BF16),
            vmem((tokens, 128), F32),
            vmem((tokens, 128), F32),
            vmem((pool + migrations,) + page, BF16),
            vmem((others * CAP,) + page, BF16),
            vmem((others * CAP,) + page, BF16),
            vmem((requests, tree, 128), F32),
            vmem((requests, 8, tree), F32),
            vmem((requests, rows, 128), BF16),
            vmem((tokens + 128 - tree, 256), BF16),
            vmem((2, rows, span), F32),
            vmem((2, span, 128), BF16),
            vmem((requests, rows, 128), F32),
            vmem((requests + 2, rows, 128), F32),
            vmem((2, rows, 128), BF16),
            vmem((2, rows, 128), BF16),
            vmem((2, rows, 128), BF16),
            vmem((2, rows, 128), BF16),
            vmem((8, 128), F32),
            vmem((8, 128), F32),
            vmem((8 * requests, 256), F32),
            dma((10,)),
            dma((6,)),
            dma((3 * PARTS + 4 * PARTS,)),
            dma((share, PARTS)),
            dma,
            dma,
            dma,
            dma,
            dma((3,)),
            dma((3,)),
            pltpu.SemaphoreType.REGULAR,
        ],
        compiler_params=pltpu.CompilerParams(
            collective_id=0, has_side_effects=True, vmem_limit_bytes=56 << 20
        ),
        name="tree_attention",
    )(
        page_table, cache_len, pair_slot, accept_node, far_len.T, far_table, mig_src[None, :], mig_page[None, :],
        norm_gain.reshape(blocks, 128), tree_parent, hidden.T, kv_pages.reshape((pool,) + page), q_weight,
        k_weight, v_weight,
    )
    out, path = pl.pallas_call(
        deliver,
        out_shape=(
            jax.ShapeDtypeStruct(out.shape, BF16),
            jax.ShapeDtypeStruct(path.shape, BF16),
        ),
        in_specs=[pl.BlockSpec(memory_space=pltpu.VMEM)] * 2,
        out_specs=(pl.BlockSpec(memory_space=pl.ANY),) * 2,
        scratch_shapes=[dma((2,))],
        name="deliver",
    )(out, path)
    return out, path[:, None, :]


def solution(mesh):
    in_specs = (
        P("grp", "tp"),
        P(),
        P(None, "tp"),
        P(None, "tp"),
        P(None, "tp"),
        P("grp", None, "tp", None),
        P("grp", None),
        P("grp"),
        P("grp", None),
        P("grp"),
        P("grp", None),
        P(),
        P("grp", None),
        P("grp"),
        P("grp"),
    )
    out_specs = (P("grp", "tp"), P("grp", "tp", None))
    return jax.shard_map(
        functools.partial(body, mesh), mesh=mesh, in_specs=in_specs, out_specs=out_specs, check_vma=False
    )
```

```python
import functools

import jax
import jax.numpy as jnp
from jax import lax
from jax.experimental import pallas as pl
from jax.experimental.pallas import tpu as pltpu
from jax.sharding import PartitionSpec as P

CAP = 4
ACCEPT = 5
THETA_LOG = 9.210340371976184
PRE = 144.0 ** (-0.5) / 50.0
POST = 50.0 * 1.4426950408889634
PARTS = 4
ITEM_PAGES = 64
EARLY = 4
F32 = jnp.float32
BF16 = jnp.bfloat16
I32 = jnp.int32
MESH = pl.DeviceIdType.MESH


def nt(a, b):
    return lax.dot_general(a, b, (((1,), (1,)), ((), ())), preferred_element_type=F32)


def nn(a, b):
    return lax.dot_general(a, b, (((1,), (0,)), ((), ())), preferred_element_type=F32)


def tn(a, b):
    return lax.dot_general(a, b, (((0,), (0,)), ((), ())), preferred_element_type=F32)


def weigh(scores):
    return jnp.exp2(jnp.tanh(scores * PRE) * POST)


def kernel(
    groups, share,
    table_hbm, lens_hbm, pair_hbm, leaf_hbm, far_len_hbm, far_table_hbm, src_hbm, page_hbm, gain_hbm, parents_hbm,
    hidden, kv_hbm, q_hbm, k_hbm, v_hbm,
    out, path,
    table, lens, pair, leaf, far_len, far_table, own_src, own_page, gain_rows, parents,
    tables, landed, wish, wish_smem, gain, xbuf, weights, acc, squares, xs, cosine, sine, pages, packed, arrived,
    masks, pickers, queries, fresh, scores, values, mixed, sums, far_query, far_ask, far_reply, far_back, row_reply,
    row_back, chain,
    small_sem, local_sem, send_sem, recv_sem, table_send, table_recv, page_send, page_recv, far_send, far_recv, passed,
):
    group = lax.axis_index("grp")
    me = lax.axis_index("tp")
    chips = share // 2
    chip, core = me // 2, me % 2
    right = ((chip + 1) % chips) * 2 + core
    left = ((chip + chips - 1) % chips) * 2 + core
    across = ((chip + 2) % chips) * 2 + core
    sibling = chip * 2 + 1 - core
    others = groups - 1
    mate = group + 1 - 2 * (group % 2)
    width, tokens = hidden.shape
    piece = width // PARTS
    pool, size = kv_hbm.shape[0:2]
    requests, tree = parents.shape
    migrations = own_src.shape[1]

    small = [
        pltpu.make_async_copy(source, target, small_sem.at[number])
        for number, (source, target) in enumerate(
            (
                (src_hbm, own_src),
                (page_hbm, own_page),
                (gain_hbm, gain_rows),
                (parents_hbm, parents),
                (table_hbm, table),
                (lens_hbm, lens),
                (pair_hbm, pair),
                (leaf_hbm, leaf),
                (far_len_hbm, far_len),
                (far_table_hbm, far_table),
            )
        )
    ]
    loads = [
        pltpu.make_async_copy(hidden, xbuf.at[me], local_sem.at[0]),
        pltpu.make_async_copy(kv_hbm, pages.at[pl.ds(0, pool)], local_sem.at[1]),
        pltpu.make_async_copy(q_hbm, weights.at[:, pl.ds(0, 256)], local_sem.at[2]),
        pltpu.make_async_copy(k_hbm, weights.at[:, pl.ds(256, 128)], local_sem.at[3]),
        pltpu.make_async_copy(v_hbm, weights.at[:, pl.ds(384, 128)], local_sem.at[4]),
    ]
    for copy in small[0:2] + loads[1:2] + loads[0:1] + loads[2:] + small[2:]:
        copy.start()

    barrier = pltpu.get_barrier_semaphore()
    for peer in (left // 2, right // 2):
        pl.semaphore_signal(barrier, inc=1, device_id=(group, peer * 2), device_id_type=MESH)

    @pl.when(core == 1)
    def _():
        pl.semaphore_signal(barrier, inc=1, device_id=(group, sibling), device_id_type=MESH)

    def ahead_of(number):
        peer = group + 1 + number
        return jnp.where(peer >= groups, peer - groups, peer)

    def behind_of(number):
        peer = group - 1 - number
        return jnp.where(peer < 0, peer + groups, peer)

    def greet():
        for number in range(others):
            peer = (ahead_of(number), chip * 2 + 1)
            pl.semaphore_signal(barrier, inc=1, device_id=peer, device_id_type=MESH)

    greet()

    @pl.when(core == 0)
    def _():
        pl.semaphore_wait(barrier, 5)
        pl.semaphore_signal(passed, inc=1, device_id=(group, sibling), device_id_type=MESH)

    @pl.when(core == 1)
    def _():
        pl.semaphore_wait(passed, 1)

    sent = []

    def send(source, owner, part, peer):
        copy = pltpu.make_async_remote_copy(
            src_ref=source,
            dst_ref=xbuf.at[owner, pl.ds(part * piece, piece)],
            send_sem=send_sem.at[len(sent)],
            recv_sem=recv_sem.at[owner, part],
            device_id=(group, peer),
            device_id_type=MESH,
        )
        copy.start()
        sent.append(copy)

    def own_part(part):
        return hidden.at[pl.ds(part * piece, piece)]

    def held(owner, part):
        return xbuf.at[owner, pl.ds(part * piece, piece)]

    def arrive(owner, part):
        pltpu.make_async_remote_copy(
            src_ref=held(owner, part),
            dst_ref=held(owner, part),
            send_sem=send_sem.at[0],
            recv_sem=recv_sem.at[owner, part],
            device_id=(group, sibling),
            device_id_type=MESH,
        ).wait_recv()

    def table_copy(number):
        return pltpu.make_async_remote_copy(
            src_ref=tables,
            dst_ref=landed.at[number],
            send_sem=table_send,
            recv_sem=table_recv,
            device_id=(ahead_of(number), me),
            device_id_type=MESH,
        )

    for part in range(PARTS):
        send(own_part(part), me, part, right)
        send(own_part(PARTS - 1 - part), me, PARTS - 1 - part, left)
    for part in range(PARTS):
        send(own_part(part), me, part, sibling)
    small[0].wait()
    small[1].wait()
    tables[:, 0:migrations] = own_src[...]
    tables[:, migrations : 2 * migrations] = own_page[...]

    def blank():
        acc[...] = jnp.zeros_like(acc)
        squares[...] = jnp.zeros_like(squares)
        fresh[...] = jnp.zeros_like(fresh)
        row_reply[...] = jnp.zeros_like(row_reply)

    pages[pl.ds(pool, migrations)] = jnp.zeros((migrations,) + pages.shape[1:], BF16)

    @pl.when(core == 1)
    def _():
        pl.semaphore_wait(barrier, 2 * others)
        pl.semaphore_signal(passed, inc=1, device_id=(group, sibling), device_id_type=MESH)

    @pl.when(core == 0)
    def _():
        pl.semaphore_wait(passed, 1)

    for number in range(others):
        table_copy(number).start()
    table_all = pltpu.make_async_remote_copy(
        src_ref=landed,
        dst_ref=landed,
        send_sem=table_send,
        recv_sem=table_recv,
        device_id=(mate, me),
        device_id_type=MESH,
    )
    table_all.wait_recv()
    every = jnp.concatenate([landed[number] for number in range(others)] + [tables[...]], 0)
    wide_lane = lax.broadcasted_iota(I32, (groups, 128), 1)

    def before(marks):
        total = marks
        for shift in (1, 2, 4, 8, 16, 32):
            total = total + jnp.where(wide_lane >= shift, pltpu.roll(total, shift, 1), 0)
        return total - marks

    def across_lanes(value):
        for shift in (64, 32, 16, 8, 4, 2, 1):
            value = value + pltpu.roll(value, shift, 1)
        return value

    hits = jnp.where((every == group) & (wide_lane < migrations), 1, 0)
    ranks = before(hits)
    asked = pltpu.roll(every, migrations, 1)
    wanted = jnp.zeros((groups, 128), I32)
    for slot in range(CAP):
        chosen = across_lanes(jnp.where((hits == 1) & (ranks == slot), asked, 0))
        wanted = jnp.where(wide_lane == slot, chosen, wanted)
    mine = jnp.broadcast_to(tables[...], (groups, 128))
    source = lax.broadcasted_iota(I32, (groups, 128), 0)
    marks = jnp.where((source == mine) & (wide_lane < migrations), 1, 0)
    spot = marks * before(marks)
    for shift in (16, 8, 4, 2, 1):
        spot = spot + pltpu.roll(spot, shift, 0)
    spot = ((mine - group + groups) % groups - 1) * CAP + spot
    spot = jnp.minimum(jnp.maximum(spot, 0), others * CAP - 1)
    wish[0:groups, :] = wanted
    wish[groups : groups + 8, :] = jnp.where(wide_lane < migrations, spot, 0)[0:8]
    move = pltpu.make_async_copy(wish, wish_smem, local_sem.at[5])
    move.start()
    move.wait()
    loads[1].wait()

    def page_copy(number):
        return pltpu.make_async_remote_copy(
            src_ref=packed.at[pl.ds(number * CAP, CAP)],
            dst_ref=arrived.at[pl.ds(number * CAP, CAP)],
            send_sem=page_send,
            recv_sem=page_recv,
            device_id=(behind_of(number), me),
            device_id_type=MESH,
        )

    for number in sorted(range(others), key=lambda step: abs(2 * step - others + 1)):
        for slot in range(CAP):
            packed[number * CAP + slot] = pages[wish_smem[number, slot]]
        page_copy(number).start()
    blank()

    for copy in small[2:]:
        copy.wait()
    blocks = gain_rows.shape[0]
    columns = jnp.transpose(jnp.concatenate([gain_rows[...], jnp.zeros((128 - blocks, 128), F32)], 0))
    for block in range(blocks):
        gain[block * 128 : block * 128 + 128, :] = jnp.broadcast_to(columns[:, block : block + 1], (128, 128))

    def consume(owner, part):
        first = owner * width + part * piece
        total = squares[...]
        for strip in range(piece // 16):
            raw = xbuf[owner, pl.ds(part * piece + strip * 16, 16), :].astype(F32)
            factor = gain[pl.ds(first + strip * 16, 16), :]
            scaled = raw * jnp.concatenate([factor] * (tokens // 128), 1)
            xs[strip * 16 : strip * 16 + 16, :] = scaled.astype(BF16)
            square = raw * raw
            total = total + (square[0:8] + square[8:16])
        squares[...] = total
        block = weights[pl.ds(pl.multiple_of(first, 16), piece), :]
        for m in range(tokens // 256):
            at = slice(m * 256, m * 256 + 256)
            acc[at, :] = acc[at, :] + tn(xs[:, at], block)

    def turn_of(i, low, low_parts, high, high_parts):
        half = len(low_parts)
        step = i % (2 * half)
        is_low = step % 2 == 0
        owner = jnp.where(is_low, low, high)
        at_low = low_parts[0] + (step // 2) * (low_parts[1] - low_parts[0])
        at_high = high_parts[0] + (step // 2) * (high_parts[1] - high_parts[0])
        part = jnp.where(is_low, at_low, at_high)
        return jnp.where(i < 2 * half, owner, owner + 1 - 2 * (owner % 2)), part

    for load in (loads[0], loads[2], loads[3], loads[4]):
        load.wait()

    def take_own(i, carry):
        consume(me, i)
        return carry

    def take_sibling(i, carry):
        arrive(sibling, i)
        consume(sibling, i)
        return carry

    lax.fori_loop(0, PARTS, take_own, 0)
    lax.fori_loop(0, PARTS, take_sibling, 0)

    def take(low, low_parts, high, high_parts):
        half = len(low_parts)

        def direct(i, carry):
            consume(*turn_of(i, low, low_parts, high, high_parts))
            return carry

        def indirect(i, carry):
            owner, part = turn_of(i, low, low_parts, high, high_parts)
            arrive(owner, part)
            consume(owner, part)
            return carry

        lax.fori_loop(0, 2 * half, direct, 0)
        lax.fori_loop(2 * half, 4 * half, indirect, 0)

    ahead, behind = tuple(range(PARTS // 2)), tuple(range(PARTS // 2, PARTS))
    for number in range(PARTS // 2):
        arrive(left, ahead[number])
        send(held(left, ahead[number]), left, ahead[number], right)
        arrive(right, behind[-1 - number])
        send(held(right, behind[-1 - number]), right, behind[-1 - number], left)
    for number in range(PARTS // 2):
        send(held(left, ahead[number]), left, ahead[number], sibling)
        send(held(right, behind[-1 - number]), right, behind[-1 - number], sibling)

    node_row = lax.broadcasted_iota(I32, (tree, tree), 0)
    node_col = lax.broadcasted_iota(I32, (tree, tree), 1)
    eye = jnp.where(node_row == node_col, 1.0, 0.0).astype(BF16)
    levels = lax.broadcasted_iota(I32, (8, tree), 0).astype(F32)
    lane = lax.broadcasted_iota(I32, (1, 128), 1)
    angle = jnp.exp((lane % 64).astype(F32) * (-THETA_LOG * 2.0 / 128.0))
    turn = jnp.where(lane < 64, -1.0, 1.0)
    side = jnp.zeros((tree, 128 - tree), F32)

    def grow(number, carry):
        for half in range(2):
            r = number * 2 + half
            up = jnp.where(node_row == parents[pl.ds(r, 1), :], 1.0, 0.0).astype(BF16) + eye
            for _ in range(2):
                up = jnp.minimum(nn(up, up), 1.0).astype(BF16)
            reached = nt(eye, up)
            masks[r] = jnp.concatenate([reached, side], 1)
            depth_row = jnp.sum(up.astype(F32), 0, keepdims=True) - 1.0
            chosen = jnp.where(node_row == jnp.full((tree, tree), leaf[r], I32), reached, 0.0)
            lineage = jnp.sum(chosen, 0, keepdims=True)
            pickers[r] = jnp.where(depth_row == levels, lineage, 0.0)
            depth = jnp.sum(reached, -1, keepdims=True) - 1.0
            base = jnp.full((1, 128), lens[r], I32)
            for j in range(2):
                base = base + jnp.where(jnp.full((1, 128), pair[0, j], I32) == r, far_len[j, group], 0)
            phase = (base.astype(F32) + depth) * angle
            rows = pl.ds(pl.multiple_of(r * tree, tree), tree)
            cosine[rows, :] = jnp.cos(phase)
            sine[rows, :] = jnp.sin(phase) * turn
        return carry

    take(left, ahead, right, behind[::-1])
    lax.fori_loop(0, requests // 2, grow, 0)
    for number in range(PARTS // 2):
        arrive(left, behind[number])
        send(held(left, behind[number]), left, behind[number], sibling)
        arrive(right, ahead[-1 - number])
        send(held(right, ahead[-1 - number]), right, ahead[-1 - number], sibling)
    take(left, behind, right, ahead[::-1])

    page_all = pltpu.make_async_remote_copy(
        src_ref=packed,
        dst_ref=arrived,
        send_sem=page_send,
        recv_sem=page_recv,
        device_id=(mate, me),
        device_id_type=MESH,
    )

    for number in range(PARTS // 2):
        arrive(across, ahead[number])
        send(held(across, ahead[number]), across, ahead[number], sibling)
        arrive(across, behind[-1 - number])
        send(held(across, behind[-1 - number]), across, behind[-1 - number], sibling)
    take(across, ahead, across, behind[::-1])

    mean = lax.dot_general(
        squares[...], jnp.full((8, 128), 1.0 / (share * width), F32), (((0,), (0,)), ((), ())),
        precision=lax.Precision.HIGHEST, preferred_element_type=F32,
    )
    scale = lax.rsqrt(mean + 1e-06)
    cosine[...] = cosine[...] * scale
    sine[...] = sine[...] * scale
    fresh[0:tokens, 128:256] = (acc[:, 384:512] * scale).astype(BF16)

    def turned(rows, at):
        value = acc[rows, at : at + 128]
        return (value * cosine[rows, :] + pltpu.roll(value, 64, 1) * sine[rows, :]).astype(BF16)

    def finish(number, carry):
        for half in range(2):
            r = number * 2 + half
            rows = pl.ds(pl.multiple_of(r * tree, tree), tree)
            fresh[rows, 0:128] = turned(rows, 256)
            queries[r, 0:tree, :] = turned(rows, 0)
            queries[r, tree : 2 * tree, :] = turned(rows, 128)
        return carry

    lax.fori_loop(0, requests // 2, finish, 0)
    for j in range(2):
        far_query[j] = queries[pair[0, j]]

    def far_copy(source, target, number):
        return pltpu.make_async_remote_copy(
            src_ref=source,
            dst_ref=target,
            send_sem=far_send.at[number],
            recv_sem=far_recv.at[number],
            device_id=(mate, me),
            device_id_type=MESH,
        )

    ask = far_copy(far_query, far_ask, 0)
    ask.start()
    page_all.wait_recv()
    for number in range(migrations):
        pages[pool + number] = arrived[wish_smem[groups, number]]

    span = ITEM_PAGES * size
    where = lax.broadcasted_iota(I32, (1, span), 1)
    items = table.shape[1] // ITEM_PAGES

    def score(query, book, row, item, at):
        both = [pages[book[row, item * ITEM_PAGES + k]] for k in range(ITEM_PAGES)]
        for k in range(ITEM_PAGES):
            values[at, k * size : k * size + size, :] = both[k][:, 128:256]
        scores[at] = nt(query, jnp.concatenate([part[:, 0:128] for part in both], 0))

    def gather_up(total, summed, valid, at):
        for part in range(span // 256):
            pieces = []
            for first in (part * 256, part * 256 + 128):
                weight = weigh(scores[at, :, first : first + 128])
                weight = jnp.where(where[:, first : first + 128] < valid, weight, 0.0)
                summed = summed + weight
                pieces.append(weight.astype(BF16))
            total = total + nn(jnp.concatenate(pieces, 1), values[at, part * 256 : part * 256 + 256, :])
        return total, summed

    def run(source, book, length_of, first, last, own, extra=None):
        def body(r, carry):
            query = source[r]
            following = jnp.minimum(r + 1, last - 1)
            length = length_of(r)
            if own:
                new = fresh[pl.ds(pl.multiple_of(r * tree, tree), 128), :]
                mask = masks[r]
                weight = weigh(nt(query, new[:, 0:128])) * jnp.concatenate([mask, mask], 0)
                summed = weight
                total = nn(weight.astype(BF16), new[:, 128:256])
                chain[pl.ds(pl.multiple_of(r * 8, 8), 8), :] = nn(pickers[r].astype(BF16), new[0:tree])
            else:
                summed = jnp.zeros((2 * tree, 128), F32)
                total = jnp.zeros((2 * tree, 128), F32)
            for item in range(items):
                if item + 1 < items:
                    score(query, book, r, item + 1, (item + 1) % 2)
                else:
                    score(source[following], book, following, 0, (item + 1) % 2)
                total, summed = gather_up(total, summed, length - item * span, item % 2)
            if own:
                mixed[r] = total
                sums[r] = summed
            else:
                far_reply[r] = total.astype(BF16)
                sums[requests + r] = summed
            if extra is not None:
                extra(r)
            return carry

        score(source[first], book, first, 0, 0)
        lax.fori_loop(first, last, body, 0)

    own_row = lax.broadcasted_iota(I32, (2 * tree, 128), 0)
    own_lane = lax.broadcasted_iota(I32, (2 * tree, 128), 1)

    def settle(r):
        total = mixed[r]
        summed = jnp.sum(sums[r], -1, keepdims=True)
        for j in range(2):
            this = jnp.full((1, 128), pair[0, j], I32) == r
            total = total + jnp.where(this, far_back[j].astype(F32), 0.0)
            spread = jnp.where((own_row == own_lane) & this, row_back[j : j + 1, :], 0.0)
            summed = summed + jnp.sum(spread, -1, keepdims=True)
        final = (total / summed).astype(BF16)
        rows = pl.ds(pl.multiple_of(r * tree, tree), tree)
        out[rows, 0:128] = final[0:tree]
        out[rows, 128:256] = final[tree : 2 * tree]

    run(queries, table, lambda r: lens[r], 0, EARLY, True)
    ask.wait_recv()
    run(far_ask, far_table, lambda r: far_len[r, mate], 0, 2, False)
    for j in range(2):
        summed = jnp.sum(sums[requests + j], -1, keepdims=True)
        row_reply[j : j + 1, :] = jnp.sum(jnp.where(own_row == own_lane, summed, 0.0), 0, keepdims=True)
    replies = far_copy(far_reply, far_back, 1), far_copy(row_reply, row_back, 2)
    for copy in replies:
        copy.start()
    late = 4
    run(queries, table, lambda r: lens[r], EARLY, requests - late, True)
    for copy in replies:
        copy.wait_recv()
    older = (requests - late) // late

    def catch_up(r):
        for number in range(older):
            settle((r - (requests - late)) * older + number)

    run(queries, table, lambda r: lens[r], requests - late, requests, True, catch_up)
    row_of = lax.broadcasted_iota(I32, path.shape[0:1] + (8 * requests,), 0)
    place = lax.broadcasted_iota(I32, path.shape[0:1] + (8 * requests,), 1)
    compact = jnp.where(place == row_of // ACCEPT * 8 + row_of % ACCEPT, 1.0, 0.0).astype(BF16)
    path[...] = nn(compact, chain[...].astype(BF16)).astype(BF16)
    for number in range(late):
        settle(requests - late + number)

    ask.wait_send()
    for copy in replies:
        copy.wait_send()
    for copy in sent:
        copy.wait_send()
    page_all.wait_send()
    table_all.wait_send()


def deliver(out, path, out_final, path_final, sems):
    copies = (
        pltpu.make_async_copy(out, out_final, sems.at[0]),
        pltpu.make_async_copy(path, path_final, sems.at[1]),
    )
    for copy in copies:
        copy.start()
    for copy in copies:
        copy.wait()


def body(
    mesh, hidden, norm_gain, q_weight, k_weight, v_weight, kv_pages, page_table, cache_len, tree_parent,
    accept_node, pair_slot, far_len, far_table, mig_src, mig_page,
):
    requests, tree = tree_parent.shape
    pool, page_size, _, entry = kv_pages.shape
    page = (page_size, entry)
    tokens, width = hidden.shape
    groups, share = mesh.shape["grp"], mesh.shape["tp"]
    migrations = mig_src.shape[0]
    others = groups - 1
    blocks = norm_gain.shape[0] // 128
    span = ITEM_PAGES * page_size
    rows = 2 * tree
    dma = pltpu.SemaphoreType.DMA
    vmem, smem = pltpu.VMEM, pltpu.SMEM
    out, path = pl.pallas_call(
        functools.partial(kernel, groups, share),
        out_shape=(
            jax.ShapeDtypeStruct((tokens, 256), BF16),
            jax.ShapeDtypeStruct((requests * ACCEPT, 256), BF16),
        ),
        in_specs=[pl.BlockSpec(memory_space=pl.ANY)] * 15,
        out_specs=(pl.BlockSpec(memory_space=pltpu.VMEM),) * 2,
        scratch_shapes=[
            smem(page_table.shape, I32),
            smem(cache_len.shape, I32),
            smem(pair_slot.shape, I32),
            smem(accept_node.shape, I32),
            smem(far_len.shape[::-1], I32),
            smem(far_table.shape, I32),
            vmem((1, migrations), I32),
            vmem((1, migrations), I32),
            vmem((blocks, 128), F32),
            vmem(tree_parent.shape, I32),
            vmem((1, 2 * migrations), I32),
            vmem((others, 1, 2 * migrations), I32),
            vmem((groups + 8, 128), I32),
            smem((groups + 8, 128), I32),
            vmem((share * width, 128), F32),
            vmem((share, width, tokens), BF16),
            vmem((share * width, 512), BF16),
            vmem((tokens, 512), F32),
            vmem((8, tokens), F32),
            vmem((width // PARTS, tokens), BF16),
            vmem((tokens, 128), F32),
            vmem((tokens, 128), F32),
            vmem((pool + migrations,) + page, BF16),
            vmem((others * CAP,) + page, BF16),
            vmem((others * CAP,) + page, BF16),
            vmem((requests, tree, 128), F32),
            vmem((requests, 8, tree), F32),
            vmem((requests, rows, 128), BF16),
            vmem((tokens + 128 - tree, 256), BF16),
            vmem((2, rows, span), F32),
            vmem((2, span, 128), BF16),
            vmem((requests, rows, 128), F32),
            vmem((requests + 2, rows, 128), F32),
            vmem((2, rows, 128), BF16),
            vmem((2, rows, 128), BF16),
            vmem((2, rows, 128), BF16),
            vmem((2, rows, 128), BF16),
            vmem((8, 128), F32),
            vmem((8, 128), F32),
            vmem((8 * requests, 256), F32),
            dma((10,)),
            dma((6,)),
            dma((3 * PARTS + 4 * PARTS,)),
            dma((share, PARTS)),
            dma,
            dma,
            dma,
            dma,
            dma((3,)),
            dma((3,)),
            pltpu.SemaphoreType.REGULAR,
        ],
        compiler_params=pltpu.CompilerParams(
            collective_id=0, has_side_effects=True, vmem_limit_bytes=56 << 20
        ),
        name="tree_attention",
    )(
        page_table, cache_len, pair_slot, accept_node, far_len.T, far_table, mig_src[None, :], mig_page[None, :],
        norm_gain.reshape(blocks, 128), tree_parent, hidden.T, kv_pages.reshape((pool,) + page), q_weight,
        k_weight, v_weight,
    )
    out, path = pl.pallas_call(
        deliver,
        out_shape=(
            jax.ShapeDtypeStruct(out.shape, BF16),
            jax.ShapeDtypeStruct(path.shape, BF16),
        ),
        in_specs=[pl.BlockSpec(memory_space=pltpu.VMEM)] * 2,
        out_specs=(pl.BlockSpec(memory_space=pl.ANY),) * 2,
        scratch_shapes=[dma((2,))],
        name="deliver",
    )(out, path)
    return out, path[:, None, :]


def solution(mesh):
    in_specs = (
        P("grp", "tp"),
        P(),
        P(None, "tp"),
        P(None, "tp"),
        P(None, "tp"),
        P("grp", None, "tp", None),
        P("grp", None),
        P("grp"),
        P("grp", None),
        P("grp"),
        P("grp", None),
        P(),
        P("grp", None),
        P("grp"),
        P("grp"),
    )
    out_specs = (P("grp", "tp"), P("grp", "tp", None))
    return jax.shard_map(
        functools.partial(body, mesh), mesh=mesh, in_specs=in_specs, out_specs=out_specs, check_vma=False
    )
```
